256 devices in a mesh: dp: 16 (over z, y_hi), seq: 16 (over x, y_lo, core).
Axes of the slice: x: 4, y: 4 (y_hi: 2, y_lo: 2; y = y_hi * 2 + y_lo), z: 8, core: 2. Of those that a mesh axis runs over, the one named last changes fastest.
Arguments:
- queries: bfloat16 [16, 3072, 512], P('dp', 'seq'), may hold values from -7 to 7
- key_rows: bfloat16 [16, 3072, 512], P('dp', 'seq'), may hold values from -7 to 7
- values: bfloat16 [16, 3072, 1536], P('dp', 'seq'), may hold values from -6 to 6
- out_proj: bfloat16 [1536, 768], replicated, may hold values from -0.15625 to 0.15625
- stream: bfloat16 [16, 3072, 768], P('dp', 'seq'), may hold values from -6 to 6
- cotangent: bfloat16 [16, 3072, 768], P('dp', 'seq'), may hold values from -6 to 6
- conv_weight: bfloat16 [3, 768, 768], replicated, may hold values from -0.125 to 0.125
Outputs:
- query_grad: bfloat16 [16, 3072, 512], P('dp', 'seq')
- key_grad: bfloat16 [16, 3072, 512], P('dp', 'seq')
- value_grad: bfloat16 [16, 3072, 1536], P('dp', 'seq')
- stream_grad: bfloat16 [16, 3072, 768], P('dp', 'seq')
- weight_grad: float32 [3, 768, 768], P(None, 'seq', 'dp')
The draws below stay inside these ranges and needn't reach their ends.
All inputs are finite; a program needn't handle non-finite values.
Results may differ from the reference program's by a relative error of at most 0.033.
Values may be sent and summed in bfloat16 or wider, within the bound.
No kernel may reach another device: no remote copies, remote signals or barrier semaphores. Data moves between devices by JAX's collectives and lax.ppermute only.
A program may use at most 256 MiB of HBM per device.

```python
import math
import jax
import jax.numpy as jnp
from jax import lax

HEADS = 8
KEY = 64
VAL = 192
CONV_CHANNELS = 768
B_DEV = 192
SEQS = 16
SEQUENCE_BINS = 3072
DILATION_BINS = 768
N_SEQ = 16


def draw_queries(key, part):
    drawn = 1.4 * jax.random.normal(jax.random.fold_in(key, 1), (SEQS, SEQUENCE_BINS, HEADS * KEY), jnp.float32)
    return jnp.clip(drawn, -7.0, 7.0).astype(jnp.bfloat16)


def draw_key_rows(key, part):
    drawn = 1.4 * jax.random.normal(jax.random.fold_in(key, 2), (SEQS, SEQUENCE_BINS, HEADS * KEY), jnp.float32)
    return jnp.clip(drawn, -7.0, 7.0).astype(jnp.bfloat16)


def levels(stream_key, extent, cuts, smallest, high):
    factor_of, own = 1.0, jax.random.fold_in(stream_key, 6)
    for position, parts in cuts:
        steps = jnp.exp(jax.random.uniform(jax.random.fold_in(own, position), (parts,), jnp.float32, smallest / len(cuts), high / len(cuts)))
        factor_of = factor_of * jnp.repeat(steps, extent[position] // parts).reshape([-1 if axis == position else 1 for axis in range(len(extent))])
    return factor_of


def gaussian(rng, extent, scale, bound, cuts=(), dtype=jnp.bfloat16):
    result = jax.random.normal(rng, extent, jnp.float32) * scale
    if len(cuts) > 0:
        result = levels(rng, extent, cuts, -0.22, 0.18) * result
    return jnp.clip(result, min=-bound, max=bound).astype(dtype)


def setup_inputs(seed: int = 0) -> dict:
    keys = jax.random.split(jax.random.key(seed), 8)
    queries = draw_queries(jax.random.fold_in(keys[7], 71), 0)
    key_rows = draw_key_rows(jax.random.fold_in(keys[7], 71), 0)
    values = gaussian(keys[2], (SEQS, SEQUENCE_BINS, HEADS * VAL), 1.0, 6.0, ((0, 16), (1, 16)))
    out_proj = gaussian(keys[3], (HEADS * VAL, CONV_CHANNELS), (HEADS * VAL) ** -0.5, 0.15625)
    stream = gaussian(keys[4], (SEQS, SEQUENCE_BINS, CONV_CHANNELS), 1.0, 6.0, ((0, 16), (1, 16)))
    cotangent = gaussian(keys[5], (SEQS, SEQUENCE_BINS, CONV_CHANNELS), 1.0, 6.0, ((0, 16), (1, 16)))
    conv_weight = gaussian(keys[6], (3, CONV_CHANNELS, CONV_CHANNELS), (3 * CONV_CHANNELS) ** -0.5, 0.125)
    return dict(queries=queries, key_rows=key_rows, values=values, out_proj=out_proj, stream=stream, cotangent=cotangent, conv_weight=conv_weight)


def gelu_pieces(inputs):
    wide = inputs.astype(jnp.float32)
    normal_cdf = 0.5 * (1.0 + jax.scipy.special.erf(wide * (1.0 / math.sqrt(2.0))))
    density = jnp.exp(-0.5 * wide * wide) * (1.0 / math.sqrt(2.0 * math.pi))
    return (wide * normal_cdf, normal_cdf + wide * density)

def block_probs(query_block, key_seq):
    query_heads = query_block.astype(jnp.float32).reshape(query_block.shape[0], HEADS, KEY)
    key_heads = key_seq.astype(jnp.float32).reshape(key_seq.shape[0], HEADS, KEY)
    scores = jnp.einsum('bhd,lhd->hbl', query_heads, key_heads) * (1.0 / math.sqrt(KEY))
    exponent = jnp.exp(scores - lax.optimization_barrier(jnp.max(scores, axis=2, keepdims=True)))
    return exponent / lax.optimization_barrier(jnp.sum(exponent, axis=2, keepdims=True))

def contract_rows(left, right):
    return lax.dot_general(left, right, (((1,), (1,)), ((), ())), preferred_element_type=jnp.float32)

def contract_bins(left, right):
    return lax.dot_general(left, right, (((0,), (0,)), ((), ())), preferred_element_type=jnp.float32)

def one_sequence(query_seq, key_seq, value_seq, stream_seq, sequence_cotangent, out_proj, conv_weight):
    score_scale = 1.0 / math.sqrt(KEY)
    query_blocks = query_seq.reshape(N_SEQ, B_DEV, HEADS * KEY)
    value_heads = value_seq.astype(jnp.float32).reshape(SEQUENCE_BINS, HEADS, VAL)
    key_heads = key_seq.astype(jnp.float32).reshape(SEQUENCE_BINS, HEADS, KEY)

    def forward_block(query_block):
        prob_half = lax.optimization_barrier(block_probs(query_block, key_seq).astype(jnp.bfloat16))
        attended_block = jnp.einsum('hbl,lhe->bhe', prob_half.astype(jnp.float32), value_heads)
        return attended_block.astype(jnp.bfloat16).reshape(B_DEV, HEADS * VAL)
    attended = lax.map(forward_block, query_blocks).reshape(SEQUENCE_BINS, HEADS * VAL)
    stream_in = (stream_seq.astype(jnp.float32) + jnp.dot(attended, out_proj, preferred_element_type=jnp.float32)).astype(jnp.bfloat16)
    activated, gelu_slope = gelu_pieces(stream_in)
    activated = activated.astype(jnp.bfloat16)
    empty_padding = jnp.zeros((DILATION_BINS, CONV_CHANNELS), jnp.bfloat16)
    gradient_forward_shift = jnp.concatenate([sequence_cotangent[DILATION_BINS:], empty_padding], axis=0)
    gradient_backward_shift = jnp.concatenate([empty_padding, sequence_cotangent[:SEQUENCE_BINS - DILATION_BINS]], axis=0)
    branch = contract_rows(gradient_forward_shift, conv_weight[0]) + contract_rows(sequence_cotangent, conv_weight[1]) + contract_rows(gradient_backward_shift, conv_weight[2])
    stream_grad = (sequence_cotangent.astype(jnp.float32) + gelu_slope * branch).astype(jnp.bfloat16)
    weight_part = jnp.stack([contract_bins(activated, gradient_forward_shift), contract_bins(activated, sequence_cotangent), contract_bins(activated, gradient_backward_shift)])
    out_grad = contract_rows(stream_grad, out_proj).astype(jnp.bfloat16)
    out_blocks = out_grad.reshape(N_SEQ, B_DEV, HEADS * VAL)
    attended_blocks = attended.reshape(N_SEQ, B_DEV, HEADS * VAL)

    def backward_block(carried, pieces):
        query_block, out_block, attended_block = pieces
        prob_full = block_probs(query_block, key_seq)
        prob_half = lax.optimization_barrier(prob_full.astype(jnp.bfloat16)).astype(jnp.float32)
        out_heads = out_block.astype(jnp.float32).reshape(B_DEV, HEADS, VAL)
        row_delta = lax.optimization_barrier(jnp.sum(out_heads * attended_block.astype(jnp.float32).reshape(B_DEV, HEADS, VAL), axis=2))
        prob_grad = jnp.einsum('bhe,lhe->hbl', out_heads, value_heads)
        score_grad = lax.optimization_barrier((prob_full * (prob_grad - row_delta.T[:, :, None])).astype(jnp.bfloat16)).astype(jnp.float32)
        query_heads = query_block.astype(jnp.float32).reshape(B_DEV, HEADS, KEY)
        query_grad = (jnp.einsum('hbl,lhd->bhd', score_grad, key_heads) * score_scale).astype(jnp.bfloat16).reshape(B_DEV, HEADS * KEY)
        key_part = (jnp.einsum('hbl,bhd->lhd', score_grad, query_heads) * score_scale).astype(jnp.bfloat16).reshape(SEQUENCE_BINS, HEADS * KEY)
        value_part = jnp.einsum('hbl,bhe->lhe', prob_half, out_heads).astype(jnp.bfloat16).reshape(SEQUENCE_BINS, HEADS * VAL)
        joined = lax.optimization_barrier(jnp.concatenate([key_part, value_part], axis=1))
        return (carried + joined.astype(jnp.float32), query_grad)
    zero_sum = jnp.zeros((SEQUENCE_BINS, HEADS * (KEY + VAL)), jnp.float32)
    summed, query_grads = lax.scan(backward_block, zero_sum, (query_blocks, out_blocks, attended_blocks))
    key_grad = summed[:, :HEADS * KEY].astype(jnp.bfloat16)
    value_grad = summed[:, HEADS * KEY:].astype(jnp.bfloat16)
    return (query_grads.reshape(SEQUENCE_BINS, HEADS * KEY), key_grad, value_grad, stream_grad, weight_part)

def reference(queries, key_rows, values, out_proj, stream, cotangent, conv_weight):

    def per_sequence(pieces):
        query_seq, key_seq, value_seq, stream_seq, sequence_cotangent = pieces
        return one_sequence(query_seq, key_seq, value_seq, stream_seq, sequence_cotangent, out_proj, conv_weight)
    query_grad, key_grad, value_grad, stream_grad, weight_parts = lax.map(per_sequence, (queries, key_rows, values, stream, cotangent))
    weight_grad = lax.optimization_barrier(jnp.sum(weight_parts, axis=0)) * (1.0 / SEQS)
    return (query_grad, key_grad, value_grad, stream_grad, weight_grad)
```

```python
import math

import jax
import jax.numpy as jnp
from jax import lax
from jax.experimental import pallas as pl
from jax.experimental.pallas import tpu as pltpu
from jax.sharding import PartitionSpec as P

HEADS = 8
KEY = 64
VAL = 192
WIDE = VAL + KEY
LOG2E = math.log2(math.e)
BF = jnp.bfloat16
F32 = jnp.float32
MIB = 1024 * 1024


def rows_by_rows(left, right):
    return lax.dot_general(left, right, (((1,), (1,)), ((), ())), preferred_element_type=F32)


def plain(left, right):
    return lax.dot_general(left, right, (((1,), (0,)), ((), ())), preferred_element_type=F32)


def call(body, outs, scratch, vmem_mib, flops, nbytes, exps, name, far_in=(), far_out=()):
    vmem = pl.BlockSpec(memory_space=pltpu.VMEM)
    far = pl.BlockSpec(memory_space=pl.ANY)
    outs = tuple(outs)

    def run(*arrays):
        got = pl.pallas_call(
            body,
            out_shape=outs,
            in_specs=[far if i in far_in else vmem for i in range(len(arrays))],
            out_specs=tuple(far if i in far_out else vmem for i in range(len(outs))),
            scratch_shapes=list(scratch),
            compiler_params=pltpu.CompilerParams(vmem_limit_bytes=vmem_mib * MIB),
            cost_estimate=pl.CostEstimate(flops=flops, bytes_accessed=nbytes, transcendentals=exps),
            name=name,
        )(*arrays)
        return got if len(outs) > 1 else got[0]

    return run


def side_by_side(block, parts):
    rows = block.shape[0] // parts
    return jnp.concatenate([block[i * rows : (i + 1) * rows] for i in range(parts)], axis=1)


def on_top(block, parts):
    width = block.shape[1] // parts
    return jnp.concatenate([block[:, i * width : (i + 1) * width] for i in range(parts)], axis=0)


def pack_body(q_ref, k_ref, v_ref, out_ref):
    rows = q_ref.shape[0]
    for h in range(HEADS):
        out_ref[h, :rows, :VAL] = v_ref[:, h * VAL : (h + 1) * VAL]
        out_ref[h, :rows, VAL:] = k_ref[:, h * KEY : (h + 1) * KEY]
        part = q_ref[:, h * KEY : (h + 1) * KEY].astype(F32) * (1.0 / math.sqrt(KEY))
        out_ref[h, rows:, :] = side_by_side(part, 4).astype(BF)


def key_tiles(own_ref, oth_ref, count=2):
    chips = own_ref.shape[0]
    rows, step = own_ref.shape[1] * 4 // 5, chips // count
    return [
        (
            side,
            t * step,
            step,
            lambda r=ref, t=t: r[t * step : (t + 1) * step, :rows, :].reshape(step * rows, WIDE),
        )
        for side, ref in enumerate((own_ref, oth_ref))
        for t in range(count)
    ]


def forward_body(own_ref, oth_ref, q_ref, att_ref, lse_ref, send_ref, score_ref):
    block = score_ref.shape[0]
    chips = own_ref.shape[0]
    rows = own_ref.shape[1] * 4 // 5
    mine = chips * rows
    for c in range(chips):
        query = on_top(own_ref[c, rows:, :].astype(F32), 4)
        padded = jnp.concatenate([jnp.zeros((rows, VAL), F32), query], axis=1)
        q_ref[c * rows : (c + 1) * rows, :] = padded.astype(BF)
    tiles = key_tiles(own_ref, oth_ref)
    tile = 2 * mine // len(tiles)

    def step(b, _):
        at = pl.ds(pl.multiple_of(b * block, block), block)
        query = q_ref[at, :]
        top = None
        for j, (_, _, _, part) in enumerate(tiles):
            scores = rows_by_rows(query, part())
            score_ref[:, j * tile : (j + 1) * tile] = scores
            high = jnp.max(scores, axis=1, keepdims=True)
            top = high if top is None else jnp.maximum(top, high)
        top = top * LOG2E
        total = jnp.zeros((block, 1), F32)
        summed = jnp.zeros((block, WIDE), F32)
        for j, (_, _, _, part) in enumerate(tiles):
            expo = jnp.exp2(score_ref[:, j * tile : (j + 1) * tile] * LOG2E - top)
            total = total + jnp.sum(expo, axis=1, keepdims=True)
            summed = summed + plain(expo.astype(BF), part())
        att_ref[at, :] = (summed * (1.0 / total)).astype(BF)
        turned = jnp.transpose(jnp.broadcast_to(top + jnp.log2(total), (block, 128)))
        lse_ref[b] = turned[:8, :]
        return 0

    lax.fori_loop(0, mine // block, step, 0)
    for c in range(chips):
        part = att_ref[c * rows : (c + 1) * rows, :].astype(F32)
        for j in range(3):
            piece = side_by_side(part[:, j * 64 : (j + 1) * 64], 4).astype(BF)
            send_ref[c, j * (rows // 4) : (j + 1) * (rows // 4), :] = piece


def probs_body(own_ref, oth_ref, q_ref, lse_ref, far_prob_ref, kt_ref, prob_ref, sems):
    blocks, _, block = lse_ref.shape
    tiles = key_tiles(own_ref, oth_ref)
    tile = prob_ref.shape[0] // len(tiles)
    for j, (_, _, _, part) in enumerate(tiles):
        here = slice(j * tile, (j + 1) * tile)
        keys = part()
        kt_ref[:, here] = jnp.transpose(keys[:, 128:].astype(F32)).astype(BF)
        for b in range(blocks):
            at = slice(b * block, (b + 1) * block)
            scores = rows_by_rows(keys, q_ref[at, :])
            prob_ref[here, at] = jnp.exp2(scores * LOG2E - lse_ref[b][:1, :]).astype(BF)
        pltpu.make_async_copy(prob_ref.at[here], far_prob_ref.at[here], sems.at[j]).start()
    for j in range(len(tiles)):
        here = slice(j * tile, (j + 1) * tile)
        pltpu.make_async_copy(prob_ref.at[here], far_prob_ref.at[here], sems.at[j]).wait()


def branch_body(cot_ref, ahead_ref, behind_ref, conv_ref, out_ref):
    ring = 4
    place = lax.axis_index("seq") // (lax.axis_size("seq") // ring)
    out_ref[...] = (
        jnp.where(place < ring - 1, rows_by_rows(ahead_ref[...], conv_ref[0]), 0.0)
        + rows_by_rows(cot_ref[...], conv_ref[1])
        + jnp.where(place > 0, rows_by_rows(behind_ref[...], conv_ref[2]), 0.0)
    )


def gelu_pieces(wide):
    normal_cdf = 0.5 * (1.0 + lax.erf(wide * (1.0 / math.sqrt(2.0))))
    density = jnp.exp(-0.5 * wide * wide) * (1.0 / math.sqrt(2.0 * math.pi))
    return (wide * normal_cdf, normal_cdf + wide * density)


def middle_body(recv_ref, proj_ref, stream_ref, cot_ref, branch_ref, grad_ref, send_ref, *rest):
    *acts, att_ref = rest
    ring = len(acts)
    place = lax.axis_index("seq") // (lax.axis_size("seq") // ring)
    quarter = recv_ref.shape[1] // 3
    for h in range(HEADS):
        for j in range(3):
            piece = recv_ref[h, j * quarter : (j + 1) * quarter, :].astype(F32)
            at = h * VAL + j * 64
            att_ref[:, at : at + 64] = on_top(piece, 4).astype(BF)
    inside = stream_ref[...].astype(F32) + plain(att_ref[...], proj_ref[...])
    activated, slope = gelu_pieces(inside.astype(BF).astype(F32))
    grad = (cot_ref[...].astype(F32) + slope * branch_ref[...]).astype(BF)
    grad_ref[...] = grad
    out_grad = rows_by_rows(grad, proj_ref[...])
    for h in range(HEADS):
        for j in range(3):
            at = h * VAL + j * 64
            piece = side_by_side(out_grad[:, at : at + 64], 4).astype(BF)
            send_ref[h, j * quarter : (j + 1) * quarter, :] = piece
    share = activated.shape[1] // ring
    blocks = [activated[:, k * share : (k + 1) * share].astype(BF) for k in range(ring)]
    for r, act_ref in enumerate(acts):
        block = blocks[0]
        for k in range(1, ring):
            block = jnp.where(lax.rem(place + r, ring) == k, blocks[k], block)
        act_ref[...] = block


def backward_body(
    own_ref,
    oth_ref,
    q_ref,
    kt_ref,
    far_prob_ref,
    att_ref,
    recv_ref,
    own_out_ref,
    oth_out_ref,
    dq_ref,
    out_ref,
    grad_ref,
    turned_ref,
    prob_ref,
    sems,
):
    def arriving(j):
        here = slice(j * tile, (j + 1) * tile)
        return pltpu.make_async_copy(far_prob_ref.at[here], prob_ref.at[here], sems.at[j])

    tiles = key_tiles(own_ref, oth_ref)
    tile = prob_ref.shape[0] // len(tiles)
    for j in range(len(tiles)):
        arriving(j).start()
    chips, rows, _ = own_out_ref.shape
    mine = chips * rows
    quarter = rows // 4
    block = 512
    for c in range(chips):
        pieces = [
            on_top(recv_ref[c, j * quarter : (j + 1) * quarter, :].astype(F32), 4) for j in range(3)
        ]
        padded = jnp.concatenate([*pieces, jnp.zeros((rows, KEY), F32)], axis=1)
        out_ref[c * rows : (c + 1) * rows, :] = padded.astype(BF)
    deltas = []
    for b in range(mine // block):
        at = slice(b * block, (b + 1) * block)
        each = out_ref[at, :].astype(F32) * att_ref[at, :].astype(F32)
        delta = jnp.sum(each, axis=1, keepdims=True)
        deltas.append(jnp.transpose(jnp.broadcast_to(delta, (block, 128)))[:1, :])
    for j, (side, first, step, part) in enumerate(tiles):
        here = slice(j * tile, (j + 1) * tile)
        keys = part()
        slot = grad_ref.at[j % 2]
        arriving(j).wait()
        for b, delta in enumerate(deltas):
            at = slice(b * block, (b + 1) * block)
            grads = rows_by_rows(keys, out_ref[at, :]) - delta
            slot[:, at] = (prob_ref[here, at].astype(F32) * grads).astype(BF)
        summed = plain(prob_ref[here, :], out_ref[...]) + plain(slot[...], q_ref[...])
        to = (own_out_ref, oth_out_ref)[side]
        to[first : first + step] = summed.astype(BF).reshape(step, rows, WIDE)
        turned = plain(kt_ref[:, here], slot[...])
        turned_ref[...] = turned if j == 0 else turned_ref[...] + turned
    scale = 1.0 / math.sqrt(KEY)
    for b in range(mine // 384):
        turned = jnp.transpose(turned_ref[:, b * 384 : (b + 1) * 384]) * scale
        for i in range(384 // rows):
            part = turned[i * rows : (i + 1) * rows, 64:]
            dq_ref[b * (384 // rows) + i] = side_by_side(part, 4).astype(BF)


def weight_body(*refs):
    ring = 4
    acts, cots, outs = refs[:ring], refs[ring : 2 * ring], refs[2 * ring : 3 * ring]
    act_ref, cot_ref = refs[3 * ring :]
    index = lax.axis_index("seq")
    stride = lax.axis_size("seq") // ring
    place, here = index // stride, index % stride
    rows, share = acts[0].shape
    for r in range(ring):
        at = pl.ds(pl.multiple_of(lax.rem(place + r, ring) * rows, rows), rows)
        act_ref[at, :] = acts[r][...]
        cot_ref[at, :] = cots[r][...]
    bins = ring * rows
    act = jnp.transpose(act_ref[...].astype(F32)).astype(BF)
    terms = (
        plain(act[:, : bins - rows], cot_ref[rows:, :]),
        plain(act, cot_ref[...]),
        plain(act[:, rows:], cot_ref[: bins - rows, :]),
    )
    piece = share // 4
    parts = [
        jnp.concatenate([t[g * piece : (g + 1) * piece] for t in terms], axis=0).astype(BF)
        for g in range(4)
    ]
    for r in range(4):
        part = parts[r]
        for g in range(1, 4):
            part = jnp.where(here == g, parts[g ^ r], part)
        outs[r][...] = part


def quarters(whole_ref, bit, outs):
    size = whole_ref.shape[0] // 4
    mine = lax.axis_index("dp") // bit % 4
    for r, out_ref in enumerate(outs):
        at = pl.ds(pl.multiple_of(jnp.bitwise_xor(mine, r) * size, size), size)
        out_ref[...] = whole_ref[at, :].astype(out_ref.dtype)


def sum_of(refs):
    both = refs[0][...].astype(F32)
    for ref in refs[1:]:
        both = both + ref[...].astype(F32)
    return both


def first_sum_body(*refs):
    refs[8][...] = jnp.transpose(sum_of(refs[:4]))
    quarters(refs[8], 4, refs[4:8])


def second_sum_body(*refs):
    refs[8][...] = sum_of(refs[:4])
    quarters(refs[8], 1, refs[4:8])


def last_sum_body(*refs):
    both = jnp.transpose(sum_of(refs[:4])) * (1.0 / lax.axis_size("dp"))
    rows = both.shape[0] // 3
    for t in range(3):
        refs[4][t] = both[t * rows : (t + 1) * rows]


def add_body(own_ref, recv_ref, dq_ref, out_ref):
    rows = own_ref.shape[1]
    for c in range(own_ref.shape[0]):
        out_ref[c, :rows, :] = (own_ref[c].astype(F32) + recv_ref[c].astype(F32)).astype(BF)
        out_ref[c, rows:, :] = dq_ref[c]


def finish_body(recv_ref, q_ref, k_ref, v_ref):
    rows = q_ref.shape[0]
    for h in range(HEADS):
        v_ref[:, h * VAL : (h + 1) * VAL] = recv_ref[h, :rows, :VAL]
        k_ref[:, h * KEY : (h + 1) * KEY] = recv_ref[h, :rows, VAL:]
        q_ref[:, h * KEY : (h + 1) * KEY] = on_top(recv_ref[h, rows:, :].astype(F32), 4).astype(BF)


def shards(queries, key_rows, values, out_proj, stream, cotangent, conv_weight):
    count = lax.axis_size("seq")
    chips = count // 2
    rows = queries.shape[1]
    channels = cotangent.shape[2]
    mine = chips * rows
    same_core = [[2 * c + p for c in range(chips)] for p in range(2)]
    partner = [(i, i ^ 1) for i in range(count)]

    def shape(*dims, dtype=BF):
        return jax.ShapeDtypeStruct(dims, dtype)

    def exchange(value):
        return lax.all_to_all(value, "seq", 0, 0, axis_index_groups=same_core, tiled=True)

    def swap(value, bit=1):
        return lax.ppermute(value, "seq", [(i, i ^ bit) for i in range(count)])

    def round_ring(value, by):
        return lax.ppermute(value, "seq", [(i, (i - by) % count) for i in range(count)])

    ring = 4
    stride = count // ring
    copies = lax.axis_size("dp")
    block = 512
    pairs_done = mine * 2 * mine
    part, quarter = 3 * channels // count, rows // 4

    packed = call(pack_body, [shape(chips, rows + quarter, WIDE)], [], 60, 0, 2 * MIB, 0, "pack")(
        queries[0], key_rows[0], values[0]
    )
    own, cot = lax.optimization_barrier((exchange(packed), cotangent[0]))
    oth = swap(own)
    cots = [round_ring(cot, by * stride) for by in (1, 2, 3)]
    query, attended, lse, send = call(
        forward_body,
        [
            shape(mine, WIDE),
            shape(mine, WIDE),
            shape(mine // block, 8, block, dtype=F32),
            shape(chips, 3 * quarter, WIDE),
        ],
        [pltpu.VMEM((block, 2 * mine), F32)],
        56,
        4 * pairs_done * WIDE,
        6 * MIB,
        pairs_done,
        "forward",
    )(own, oth)
    send, *cots = lax.optimization_barrier((send, *cots))
    recv = exchange(send)
    probs, keys_turned = call(
        probs_body,
        [shape(2 * mine, mine), shape(128, 2 * mine)],
        [pltpu.VMEM((2 * mine, mine), BF), pltpu.SemaphoreType.DMA((4,))],
        56,
        2 * pairs_done * WIDE,
        12 * MIB,
        pairs_done,
        "probs",
        far_out=(0,),
    )(own, oth, query, lse)
    branch = call(
        branch_body,
        [shape(rows, channels, dtype=F32)],
        [],
        56,
        6 * rows * channels * channels,
        5 * MIB,
        0,
        "branch",
    )(cot, cots[0], cots[2], conv_weight)
    recv, probs, branch = lax.optimization_barrier((recv, probs, branch))
    stream_grad, send, *acts = call(
        middle_body,
        [
            shape(rows, channels),
            shape(chips, 3 * quarter, WIDE),
            *[shape(rows, channels // ring)] * ring,
        ],
        [pltpu.VMEM((rows, HEADS * VAL), BF)],
        56,
        4 * rows * channels * HEADS * VAL,
        5 * MIB,
        2 * rows * channels,
        "middle",
    )(recv, out_proj, stream[0], cot, branch)
    moved = [round_ring(acts[ring - by], by * stride) for by in (1, 2, 3)]
    send, *moved = lax.optimization_barrier((send, *moved))
    recv = exchange(send)
    parts = call(
        weight_body,
        [shape(part, channels)] * 4,
        [
            pltpu.VMEM((ring * rows, channels // ring), BF),
            pltpu.VMEM((ring * rows, channels), BF),
        ],
        56,
        6 * ring * rows * channels * channels // ring,
        5 * MIB,
        0,
        "weight",
    )(acts[0], *moved, cot, *cots)
    def shared(parts, size, body, name):
        return call(
            body,
            [shape(size, part, dtype=F32)] + [shape(size, part)] * 3,
            [pltpu.VMEM((4 * size, part), F32)],
            12,
            0,
            MIB,
            0,
            name,
        )(*parts)

    def dp_swap(value, bit):
        return lax.ppermute(value, "dp", [(i, i ^ bit) for i in range(copies)])

    given = [swap(parts[r], r) for r in (1, 2, 3)]
    parts = shared([parts[0], *given], channels // 4, first_sum_body, "first_sum")
    recv, *parts = lax.optimization_barrier((recv, *parts))
    parts = [parts[0]] + [dp_swap(parts[r], 4 * r) for r in (1, 2, 3)]
    own_grad, oth_grad, dq = call(
        backward_body,
        [shape(chips, rows, WIDE), shape(chips, rows, WIDE), shape(chips, quarter, WIDE)],
        [
            pltpu.VMEM((mine, WIDE), BF),
            pltpu.VMEM((2, mine // 2, mine), BF),
            pltpu.VMEM((128, mine), F32),
            pltpu.VMEM((2 * mine, mine), BF),
            pltpu.SemaphoreType.DMA((4,)),
        ],
        56,
        8 * pairs_done * WIDE,
        16 * MIB,
        0,
        "backward",
        far_in=(4,),
    )(own, oth, query, keys_turned, probs, attended, recv)
    *parts, oth_grad = lax.optimization_barrier((*parts, oth_grad))
    swapped = swap(oth_grad)
    parts = shared(parts, channels // copies, second_sum_body, "second_sum")
    packed = call(add_body, [shape(chips, rows + quarter, WIDE)], [], 12, 0, 3 * MIB, 0, "add")(
        own_grad, swapped, dq
    )
    packed, *parts = lax.optimization_barrier((packed, *parts))
    recv = exchange(packed)
    parts = [parts[0]] + [dp_swap(parts[r], r) for r in (1, 2, 3)]
    weight_grad = call(
        last_sum_body,
        [shape(3, channels // count, channels // copies, dtype=F32)],
        [],
        12,
        0,
        MIB,
        0,
        "last_sum",
    )(*parts)
    query_grad, key_grad, value_grad = call(
        finish_body,
        [shape(rows, HEADS * KEY), shape(rows, HEADS * KEY), shape(rows, HEADS * VAL)],
        [],
        12,
        0,
        2 * MIB,
        0,
        "finish",
    )(recv)
    return (query_grad[None], key_grad[None], value_grad[None], stream_grad[None], weight_grad)


def solution(mesh):
    return jax.shard_map(
        shards,
        mesh=mesh,
        in_specs=(
            P("dp", "seq", None),
            P("dp", "seq", None),
            P("dp", "seq", None),
            P(),
            P("dp", "seq", None),
            P("dp", "seq", None),
            P(),
        ),
        out_specs=(
            P("dp", "seq", None),
            P("dp", "seq", None),
            P("dp", "seq", None),
            P("dp", "seq", None),
            P(None, "seq", "dp"),
        ),
        check_vma=False,
    )
```

```python
import math

import jax
import jax.numpy as jnp
from jax import lax
from jax.experimental import pallas as pl
from jax.experimental.pallas import tpu as pltpu
from jax.sharding import PartitionSpec as P

HEADS = 8
KEY = 64
VAL = 192
WIDE = VAL + KEY
LOG2E = math.log2(math.e)
BF = jnp.bfloat16
F32 = jnp.float32
MIB = 1024 * 1024


def rows_by_rows(left, right):
    return lax.dot_general(left, right, (((1,), (1,)), ((), ())), preferred_element_type=F32)


def plain(left, right):
    return lax.dot_general(left, right, (((1,), (0,)), ((), ())), preferred_element_type=F32)


def call(body, outs, scratch, vmem_mib, flops, nbytes, exps, name, far_in=(), far_out=()):
    vmem = pl.BlockSpec(memory_space=pltpu.VMEM)
    far = pl.BlockSpec(memory_space=pl.ANY)
    outs = tuple(outs)

    def run(*arrays):
        got = pl.pallas_call(
            body,
            out_shape=outs,
            in_specs=[far if i in far_in else vmem for i in range(len(arrays))],
            out_specs=tuple(far if i in far_out else vmem for i in range(len(outs))),
            scratch_shapes=list(scratch),
            compiler_params=pltpu.CompilerParams(vmem_limit_bytes=vmem_mib * MIB),
            cost_estimate=pl.CostEstimate(flops=flops, bytes_accessed=nbytes, transcendentals=exps),
            name=name,
        )(*arrays)
        return got if len(outs) > 1 else got[0]

    return run


def side_by_side(block, parts):
    rows = block.shape[0] // parts
    return jnp.concatenate([block[i * rows : (i + 1) * rows] for i in range(parts)], axis=1)


def on_top(block, parts):
    width = block.shape[1] // parts
    return jnp.concatenate([block[:, i * width : (i + 1) * width] for i in range(parts)], axis=0)


def pack_body(q_ref, k_ref, v_ref, out_ref):
    rows = q_ref.shape[0]
    for h in range(HEADS):
        out_ref[h, :rows, :VAL] = v_ref[:, h * VAL : (h + 1) * VAL]
        out_ref[h, :rows, VAL:] = k_ref[:, h * KEY : (h + 1) * KEY]
        part = q_ref[:, h * KEY : (h + 1) * KEY].astype(F32) * (1.0 / math.sqrt(KEY))
        out_ref[h, rows:, :] = side_by_side(part, 4).astype(BF)


def key_tiles(own_ref, oth_ref, count=2):
    chips = own_ref.shape[0]
    rows, step = own_ref.shape[1] * 4 // 5, chips // count
    return [
        (
            side,
            t * step,
            step,
            lambda r=ref, t=t: r[t * step : (t + 1) * step, :rows, :].reshape(step * rows, WIDE),
        )
        for side, ref in enumerate((own_ref, oth_ref))
        for t in range(count)
    ]


def forward_body(own_ref, oth_ref, q_ref, att_ref, lse_ref, send_ref, *score_refs):
    block = score_refs[0].shape[0]
    chips = own_ref.shape[0]
    rows = own_ref.shape[1] * 4 // 5
    mine = chips * rows
    blocks = mine // block
    for c in range(chips):
        query = on_top(own_ref[c, rows:, :].astype(F32), 4)
        padded = jnp.concatenate([jnp.zeros((rows, VAL), F32), query], axis=1)
        q_ref[c * rows : (c + 1) * rows, :] = padded.astype(BF)
    tiles = key_tiles(own_ref, oth_ref)
    tile = 2 * mine // len(tiles)

    def score(b, j, top):
        scores = rows_by_rows(q_ref[b * block : (b + 1) * block, :], tiles[j][3]())
        score_refs[b % 2][:, j * tile : (j + 1) * tile] = scores
        high = jnp.max(scores, axis=1, keepdims=True)
        return high if top is None else jnp.maximum(top, high)

    top = None
    for j in range(len(tiles)):
        top = score(0, j, top)
    for b in range(blocks):
        following = None
        top = top * LOG2E
        total = jnp.zeros((block, 1), F32)
        summed = jnp.zeros((block, WIDE), F32)
        for j, (_, _, _, part) in enumerate(tiles):
            if b + 1 < blocks:
                following = score(b + 1, j, following)
            expo = jnp.exp2(score_refs[b % 2][:, j * tile : (j + 1) * tile] * LOG2E - top)
            total = total + jnp.sum(expo, axis=1, keepdims=True)
            summed = summed + plain(expo.astype(BF), part())
        att_ref[b * block : (b + 1) * block, :] = (summed * (1.0 / total)).astype(BF)
        turned = jnp.transpose(jnp.broadcast_to(top + jnp.log2(total), (block, 128)))
        lse_ref[b] = turned[:8, :]
        top = following
    for c in range(chips):
        part = att_ref[c * rows : (c + 1) * rows, :].astype(F32)
        for j in range(3):
            piece = side_by_side(part[:, j * 64 : (j + 1) * 64], 4).astype(BF)
            send_ref[c, j * (rows // 4) : (j + 1) * (rows // 4), :] = piece


def probs_body(own_ref, oth_ref, q_ref, lse_ref, far_prob_ref, kt_ref, prob_ref, sems):
    blocks, _, block = lse_ref.shape
    tiles = key_tiles(own_ref, oth_ref)
    tile = prob_ref.shape[0] // len(tiles)
    for j, (_, _, _, part) in enumerate(tiles):
        here = slice(j * tile, (j + 1) * tile)
        keys = part()
        kt_ref[:, here] = jnp.transpose(keys[:, 128:].astype(F32)).astype(BF)
        for b in range(blocks):
            at = slice(b * block, (b + 1) * block)
            scores = rows_by_rows(keys, q_ref[at, :])
            prob_ref[here, at] = jnp.exp2(scores * LOG2E - lse_ref[b][:1, :]).astype(BF)
        pltpu.make_async_copy(prob_ref.at[here], far_prob_ref.at[here], sems.at[j]).start()
    for j in range(len(tiles)):
        here = slice(j * tile, (j + 1) * tile)
        pltpu.make_async_copy(prob_ref.at[here], far_prob_ref.at[here], sems.at[j]).wait()


def branch_body(cot_ref, ahead_ref, behind_ref, conv_ref, out_ref):
    ring = 4
    place = lax.axis_index("seq") // (lax.axis_size("seq") // ring)
    out_ref[...] = (
        jnp.where(place < ring - 1, rows_by_rows(ahead_ref[...], conv_ref[0]), 0.0)
        + rows_by_rows(cot_ref[...], conv_ref[1])
        + jnp.where(place > 0, rows_by_rows(behind_ref[...], conv_ref[2]), 0.0)
    )


def gelu_pieces(wide):
    normal_cdf = 0.5 * (1.0 + lax.erf(wide * (1.0 / math.sqrt(2.0))))
    density = jnp.exp(-0.5 * wide * wide) * (1.0 / math.sqrt(2.0 * math.pi))
    return (wide * normal_cdf, normal_cdf + wide * density)


def middle_body(recv_ref, proj_ref, stream_ref, cot_ref, branch_ref, grad_ref, send_ref, *rest):
    *acts, att_ref = rest
    ring = len(acts)
    place = lax.axis_index("seq") // (lax.axis_size("seq") // ring)
    quarter = recv_ref.shape[1] // 3
    for h in range(HEADS):
        for j in range(3):
            piece = recv_ref[h, j * quarter : (j + 1) * quarter, :].astype(F32)
            at = h * VAL + j * 64
            att_ref[:, at : at + 64] = on_top(piece, 4).astype(BF)
    inside = stream_ref[...].astype(F32) + plain(att_ref[...], proj_ref[...])
    activated, slope = gelu_pieces(inside.astype(BF).astype(F32))
    grad = (cot_ref[...].astype(F32) + slope * branch_ref[...]).astype(BF)
    grad_ref[...] = grad
    out_grad = rows_by_rows(grad, proj_ref[...])
    for h in range(HEADS):
        for j in range(3):
            at = h * VAL + j * 64
            piece = side_by_side(out_grad[:, at : at + 64], 4).astype(BF)
            send_ref[h, j * quarter : (j + 1) * quarter, :] = piece
    share = activated.shape[1] // ring
    blocks = [activated[:, k * share : (k + 1) * share].astype(BF) for k in range(ring)]
    for r, act_ref in enumerate(acts):
        block = blocks[0]
        for k in range(1, ring):
            block = jnp.where(lax.rem(place + r, ring) == k, blocks[k], block)
        act_ref[...] = block


def backward_body(*refs):
    far_recv, far_att, far_own, far_prob, far_kt, far_q, far_oth = refs[:7]
    far_own_out, far_oth_out, dq_ref = refs[7:10]
    recv_ref, att_ref, own_ref, prob_ref, kt_ref, q_ref, oth_ref = refs[10:17]
    own_out_ref, oth_out_ref, out_ref, grad_ref, turned_ref, sems = refs[17:]
    chips, rows, _ = own_out_ref.shape
    mine = chips * rows
    quarter = rows // 4
    block = 512
    tiles = key_tiles(own_ref, oth_ref)
    tile = 2 * mine // len(tiles)
    heres = [slice(j * tile, (j + 1) * tile) for j in range(len(tiles))]
    recv, att, own, kt, query, oth = [
        pltpu.make_async_copy(far, near, sems.at[i])
        for i, (far, near) in enumerate(
            (
                (far_recv, recv_ref),
                (far_att, att_ref),
                (far_own, own_ref),
                (far_kt, kt_ref),
                (far_q, q_ref),
                (far_oth, oth_ref),
            )
        )
    ]
    probs = [
        pltpu.make_async_copy(far_prob.at[here], prob_ref.at[here], sems.at[6 + j])
        for j, here in enumerate(heres)
    ]
    leaving = []
    for j, (side, first, step, _) in enumerate(tiles):
        far, near = ((far_own_out, own_out_ref), (far_oth_out, oth_out_ref))[side]
        at = slice(first, first + step)
        leaving.append(pltpu.make_async_copy(near.at[at], far.at[at], sems.at[10 + j]))
    for one in (recv, att, own, probs[0], query, kt, probs[1], oth, probs[2], probs[3]):
        one.start()
    recv.wait()
    for c in range(chips):
        pieces = [
            on_top(recv_ref[c, j * quarter : (j + 1) * quarter, :].astype(F32), 4) for j in range(3)
        ]
        padded = jnp.concatenate([*pieces, jnp.zeros((rows, KEY), F32)], axis=1)
        out_ref[c * rows : (c + 1) * rows, :] = padded.astype(BF)
    att.wait()
    deltas = []
    for b in range(mine // block):
        at = slice(b * block, (b + 1) * block)
        each = out_ref[at, :].astype(F32) * att_ref[at, :].astype(F32)
        delta = jnp.sum(each, axis=1, keepdims=True)
        deltas.append(jnp.transpose(jnp.broadcast_to(delta, (block, 128)))[:1, :])

    def score_grads(j):
        probs[j].wait()
        keys = tiles[j][3]()
        for b, delta in enumerate(deltas):
            at = slice(b * block, (b + 1) * block)
            grads = rows_by_rows(keys, out_ref[at, :]) - delta
            grad_ref[j % 2, :, at] = (prob_ref[heres[j], at].astype(F32) * grads).astype(BF)

    own.wait()
    score_grads(0)
    query.wait()
    kt.wait()
    for j, (side, first, step, _) in enumerate(tiles):
        if j + 1 < len(tiles):
            if j + 1 == len(tiles) // 2:
                oth.wait()
            score_grads(j + 1)
        slot = grad_ref[j % 2]
        summed = plain(prob_ref[heres[j], :], out_ref[...]) + plain(slot, q_ref[...])
        near = (own_out_ref, oth_out_ref)[side]
        near[first : first + step] = summed.astype(BF).reshape(step, rows, WIDE)
        leaving[j].start()
        turned = plain(kt_ref[:, heres[j]], slot)
        turned_ref[...] = turned if j == 0 else turned_ref[...] + turned
    scale = 1.0 / math.sqrt(KEY)
    for b in range(mine // 384):
        turned = jnp.transpose(turned_ref[:, b * 384 : (b + 1) * 384]) * scale
        for i in range(384 // rows):
            part = turned[i * rows : (i + 1) * rows, 64:]
            dq_ref[b * (384 // rows) + i] = side_by_side(part, 4).astype(BF)
    for one in leaving:
        one.wait()


def weight_body(*refs):
    ring = 4
    acts, cots, (out_ref, act_ref, cot_ref) = refs[:ring], refs[ring : 2 * ring], refs[2 * ring :]
    index = lax.axis_index("seq")
    stride = lax.axis_size("seq") // ring
    place, here = index // stride, index % stride
    rows, share = acts[0].shape
    for r in range(ring):
        at = pl.ds(pl.multiple_of(lax.rem(place + r, ring) * rows, rows), rows)
        act_ref[at, :] = acts[r][...]
        cot_ref[at, :] = cots[r][...]
    bins = ring * rows
    act = jnp.transpose(act_ref[...].astype(F32)).astype(BF)
    terms = (
        plain(act[:, : bins - rows], cot_ref[rows:, :]),
        plain(act, cot_ref[...]),
        plain(act[:, rows:], cot_ref[: bins - rows, :]),
    )
    piece = share // 4
    parts = [
        jnp.concatenate([t[g * piece : (g + 1) * piece] for t in terms], axis=0) for g in range(4)
    ]
    order = []
    for r in range(4):
        part = parts[r]
        for g in range(1, 4):
            part = jnp.where(here == g, parts[g ^ r], part)
        order.append(part)
    out_ref[...] = jnp.transpose(jnp.concatenate(order, axis=0)).astype(BF)


def sum_of(refs):
    both = refs[0][...].astype(F32)
    for ref in refs[1:]:
        both = both + ref[...].astype(F32)
    return both


def dp_sum_body(terms_ref, *outs):
    both = sum_of([terms_ref.at[i] for i in range(terms_ref.shape[0])])
    width = outs[0].shape[1]
    for r, out_ref in enumerate(outs):
        out_ref[...] = both[:, r * width : (r + 1) * width]


def last_sum_body(*refs):
    both = jnp.transpose(sum_of(refs[:4])) * (1.0 / lax.axis_size("dp"))
    rows = both.shape[0] // 3
    for t in range(3):
        refs[4][t] = both[t * rows : (t + 1) * rows]


def add_body(own_ref, recv_ref, dq_ref, out_ref):
    rows = own_ref.shape[1]
    for c in range(own_ref.shape[0]):
        out_ref[c, :rows, :] = (own_ref[c].astype(F32) + recv_ref[c].astype(F32)).astype(BF)
        out_ref[c, rows:, :] = dq_ref[c]


def finish_body(recv_ref, q_ref, k_ref, v_ref):
    rows = q_ref.shape[0]
    for h in range(HEADS):
        v_ref[:, h * VAL : (h + 1) * VAL] = recv_ref[h, :rows, :VAL]
        k_ref[:, h * KEY : (h + 1) * KEY] = recv_ref[h, :rows, VAL:]
        q_ref[:, h * KEY : (h + 1) * KEY] = on_top(recv_ref[h, rows:, :].astype(F32), 4).astype(BF)


def shards(queries, key_rows, values, out_proj, stream, cotangent, conv_weight):
    count = lax.axis_size("seq")
    chips = count // 2
    rows = queries.shape[1]
    channels = cotangent.shape[2]
    mine = chips * rows
    same_core = [[2 * c + p for c in range(chips)] for p in range(2)]
    partner = [(i, i ^ 1) for i in range(count)]

    def shape(*dims, dtype=BF):
        return jax.ShapeDtypeStruct(dims, dtype)

    def exchange(value):
        return lax.all_to_all(value, "seq", 0, 0, axis_index_groups=same_core, tiled=True)

    def swap(value, bit=1):
        return lax.ppermute(value, "seq", [(i, i ^ bit) for i in range(count)])

    def round_ring(value, by):
        return lax.ppermute(value, "seq", [(i, (i - by) % count) for i in range(count)])

    ring = 4
    stride = count // ring
    copies = lax.axis_size("dp")
    block = 512
    pairs_done = mine * 2 * mine
    part, quarter = 3 * channels // count, rows // 4

    packed = call(pack_body, [shape(chips, rows + quarter, WIDE)], [], 60, 0, 2 * MIB, 0, "pack")(
        queries[0], key_rows[0], values[0]
    )
    own, cot = lax.optimization_barrier((exchange(packed), cotangent[0]))
    oth = swap(own)
    cots = [round_ring(cot, by * stride) for by in (1, 2, 3)]
    query, attended, lse, send = call(
        forward_body,
        [
            shape(mine, WIDE),
            shape(mine, WIDE),
            shape(mine // block, 8, block, dtype=F32),
            shape(chips, 3 * quarter, WIDE),
        ],
        [pltpu.VMEM((block, 2 * mine), F32)] * 2,
        56,
        4 * pairs_done * WIDE,
        6 * MIB,
        pairs_done,
        "forward",
    )(own, oth)
    send, *cots = lax.optimization_barrier((send, *cots))
    recv = exchange(send)
    probs, keys_turned = call(
        probs_body,
        [shape(2 * mine, mine), shape(128, 2 * mine)],
        [pltpu.VMEM((2 * mine, mine), BF), pltpu.SemaphoreType.DMA((4,))],
        56,
        2 * pairs_done * WIDE,
        12 * MIB,
        pairs_done,
        "probs",
        far_out=(0,),
    )(own, oth, query, lse)
    branch = call(
        branch_body,
        [shape(rows, channels, dtype=F32)],
        [],
        56,
        6 * rows * channels * channels,
        5 * MIB,
        0,
        "branch",
    )(cot, cots[0], cots[2], conv_weight)
    recv, probs, branch = lax.optimization_barrier((recv, probs, branch))
    stream_grad, send, *acts = call(
        middle_body,
        [
            shape(rows, channels),
            shape(chips, 3 * quarter, WIDE),
            *[shape(rows, channels // ring)] * ring,
        ],
        [pltpu.VMEM((rows, HEADS * VAL), BF)],
        56,
        4 * rows * channels * HEADS * VAL,
        5 * MIB,
        2 * rows * channels,
        "middle",
    )(recv, out_proj, stream[0], cot, branch)
    recv = exchange(send)
    moved = [round_ring(acts[ring - by], by * stride) for by in (1, 2, 3)]
    terms = call(
        weight_body,
        [shape(channels, ring * part)],
        [
            pltpu.VMEM((ring * rows, channels // ring), BF),
            pltpu.VMEM((ring * rows, channels), BF),
        ],
        56,
        6 * ring * rows * channels * channels // ring,
        5 * MIB,
        0,
        "weight",
    )(acts[0], *moved, cot, *cots)
    recv, terms = lax.optimization_barrier((recv, terms))
    terms = terms.reshape(copies, channels // copies, ring * part)
    terms = lax.all_to_all(terms, "dp", 0, 0, tiled=True)
    ins = (recv, attended, own, probs, keys_turned, query, oth)
    own_grad, oth_grad, dq = call(
        backward_body,
        [shape(chips, rows, WIDE), shape(chips, rows, WIDE), shape(chips, quarter, WIDE)],
        [
            *[pltpu.VMEM(one.shape, one.dtype) for one in ins],
            *[pltpu.VMEM((chips, rows, WIDE), BF)] * 2,
            pltpu.VMEM((mine, WIDE), BF),
            pltpu.VMEM((2, mine // 2, mine), BF),
            pltpu.VMEM((128, mine), F32),
            pltpu.SemaphoreType.DMA((14,)),
        ],
        56,
        8 * pairs_done * WIDE,
        16 * MIB,
        0,
        "backward",
        far_in=range(7),
        far_out=(0, 1),
    )(*ins)
    terms, oth_grad = lax.optimization_barrier((terms, oth_grad))
    swapped = swap(oth_grad)
    parts = call(
        dp_sum_body,
        [shape(channels // copies, part, dtype=F32)] * ring,
        [],
        12,
        0,
        MIB,
        0,
        "dp_sum",
    )(terms)
    packed = call(add_body, [shape(chips, rows + quarter, WIDE)], [], 12, 0, 3 * MIB, 0, "add")(
        own_grad, swapped, dq
    )
    parts = [parts[0]] + [swap(parts[r], r) for r in (1, 2, 3)]
    packed, *parts = lax.optimization_barrier((packed, *parts))
    recv = exchange(packed)
    weight_grad = call(
        last_sum_body,
        [shape(3, channels // count, channels // copies, dtype=F32)],
        [],
        12,
        0,
        MIB,
        0,
        "last_sum",
    )(*parts)
    query_grad, key_grad, value_grad = call(
        finish_body,
        [shape(rows, HEADS * KEY), shape(rows, HEADS * KEY), shape(rows, HEADS * VAL)],
        [],
        12,
        0,
        2 * MIB,
        0,
        "finish",
    )(recv)
    return (query_grad[None], key_grad[None], value_grad[None], stream_grad[None], weight_grad)


def solution(mesh):
    return jax.shard_map(
        shards,
        mesh=mesh,
        in_specs=(
            P("dp", "seq", None),
            P("dp", "seq", None),
            P("dp", "seq", None),
            P(),
            P("dp", "seq", None),
            P("dp", "seq", None),
            P(),
        ),
        out_specs=(
            P("dp", "seq", None),
            P("dp", "seq", None),
            P("dp", "seq", None),
            P("dp", "seq", None),
            P(None, "seq", "dp"),
        ),
        check_vma=False,
    )
```

```python
import math

import jax
import jax.numpy as jnp
from jax import lax
from jax.experimental import pallas as pl
from jax.experimental.pallas import tpu as pltpu
from jax.sharding import PartitionSpec as P

HEADS = 8
KEY = 64
VAL = 192
WIDE = VAL + KEY
LOG2E = math.log2(math.e)
BF = jnp.bfloat16
F32 = jnp.float32
MIB = 1024 * 1024


def rows_by_rows(left, right):
    return lax.dot_general(left, right, (((1,), (1,)), ((), ())), preferred_element_type=F32)


def plain(left, right):
    return lax.dot_general(left, right, (((1,), (0,)), ((), ())), preferred_element_type=F32)


def call(body, outs, scratch, vmem_mib, flops, nbytes, exps, name, far_in=(), far_out=()):
    vmem = pl.BlockSpec(memory_space=pltpu.VMEM)
    far = pl.BlockSpec(memory_space=pl.ANY)
    outs = tuple(outs)

    def run(*arrays):
        got = pl.pallas_call(
            body,
            out_shape=outs,
            in_specs=[far if i in far_in else vmem for i in range(len(arrays))],
            out_specs=tuple(far if i in far_out else vmem for i in range(len(outs))),
            scratch_shapes=list(scratch),
            compiler_params=pltpu.CompilerParams(vmem_limit_bytes=vmem_mib * MIB),
            cost_estimate=pl.CostEstimate(flops=flops, bytes_accessed=nbytes, transcendentals=exps),
            name=name,
        )(*arrays)
        return got if len(outs) > 1 else got[0]

    return run


def side_by_side(block, parts):
    rows = block.shape[0] // parts
    return jnp.concatenate([block[i * rows : (i + 1) * rows] for i in range(parts)], axis=1)


def on_top(block, parts):
    width = block.shape[1] // parts
    return jnp.concatenate([block[:, i * width : (i + 1) * width] for i in range(parts)], axis=0)


def pack_body(q_ref, k_ref, v_ref, out_ref):
    rows = q_ref.shape[0]
    for h in range(HEADS):
        out_ref[h, :rows, :VAL] = v_ref[:, h * VAL : (h + 1) * VAL]
        out_ref[h, :rows, VAL:] = k_ref[:, h * KEY : (h + 1) * KEY]
        part = q_ref[:, h * KEY : (h + 1) * KEY].astype(F32) * (1.0 / math.sqrt(KEY))
        out_ref[h, rows:, :] = side_by_side(part, 4).astype(BF)


def key_tiles(own_ref, oth_ref, count=2):
    chips = own_ref.shape[0]
    rows, step = own_ref.shape[1] * 4 // 5, chips // count
    return [
        (
            side,
            t * step,
            step,
            lambda r=ref, t=t: r[t * step : (t + 1) * step, :rows, :].reshape(step * rows, WIDE),
        )
        for side, ref in enumerate((own_ref, oth_ref))
        for t in range(count)
    ]


def forward_body(own_ref, oth_ref, q_ref, att_ref, lse_ref, send_ref, *score_refs):
    block = score_refs[0].shape[0]
    chips = own_ref.shape[0]
    rows = own_ref.shape[1] * 4 // 5
    mine = chips * rows
    blocks = mine // block
    for c in range(chips):
        query = on_top(own_ref[c, rows:, :].astype(F32), 4)
        padded = jnp.concatenate([jnp.zeros((rows, VAL), F32), query], axis=1)
        q_ref[c * rows : (c + 1) * rows, :] = padded.astype(BF)
    tiles = key_tiles(own_ref, oth_ref)
    tile = 2 * mine // len(tiles)

    def score(b, j, top):
        scores = rows_by_rows(q_ref[b * block : (b + 1) * block, :], tiles[j][3]())
        score_refs[b % 2][:, j * tile : (j + 1) * tile] = scores
        high = jnp.max(scores, axis=1, keepdims=True)
        return high if top is None else jnp.maximum(top, high)

    top = None
    for j in range(len(tiles)):
        top = score(0, j, top)
    for b in range(blocks):
        following = None
        top = top * LOG2E
        total = jnp.zeros((block, 1), F32)
        summed = jnp.zeros((block, WIDE), F32)
        for j, (_, _, _, part) in enumerate(tiles):
            if b + 1 < blocks:
                following = score(b + 1, j, following)
            expo = jnp.exp2(score_refs[b % 2][:, j * tile : (j + 1) * tile] * LOG2E - top)
            total = total + jnp.sum(expo, axis=1, keepdims=True)
            summed = summed + plain(expo.astype(BF), part())
        att_ref[b * block : (b + 1) * block, :] = (summed * (1.0 / total)).astype(BF)
        turned = jnp.transpose(jnp.broadcast_to(top + jnp.log2(total), (block, 128)))
        lse_ref[b] = turned[:8, :]
        top = following
    for c in range(chips):
        part = att_ref[c * rows : (c + 1) * rows, :].astype(F32)
        for j in range(3):
            piece = side_by_side(part[:, j * 64 : (j + 1) * 64], 4).astype(BF)
            send_ref[c, j * (rows // 4) : (j + 1) * (rows // 4), :] = piece


def probs_body(own_ref, oth_ref, q_ref, lse_ref, far_prob_ref, kt_ref, prob_ref, sems):
    blocks, _, block = lse_ref.shape
    tiles = key_tiles(own_ref, oth_ref)
    tile = prob_ref.shape[0] // len(tiles)
    for j, (_, _, _, part) in enumerate(tiles):
        here = slice(j * tile, (j + 1) * tile)
        keys = part()
        kt_ref[:, here] = jnp.transpose(keys[:, 128:].astype(F32)).astype(BF)
        for b in range(blocks):
            at = slice(b * block, (b + 1) * block)
            scores = rows_by_rows(keys, q_ref[at, :])
            prob_ref[here, at] = jnp.exp2(scores * LOG2E - lse_ref[b][:1, :]).astype(BF)
        pltpu.make_async_copy(prob_ref.at[here], far_prob_ref.at[here], sems.at[j]).start()
    for j in range(len(tiles)):
        here = slice(j * tile, (j + 1) * tile)
        pltpu.make_async_copy(prob_ref.at[here], far_prob_ref.at[here], sems.at[j]).wait()


def branch_body(cot_ref, ahead_ref, behind_ref, conv_ref, out_ref):
    ring = 4
    place = lax.axis_index("seq") // (lax.axis_size("seq") // ring)
    out_ref[...] = (
        jnp.where(place < ring - 1, rows_by_rows(ahead_ref[...], conv_ref[0]), 0.0)
        + rows_by_rows(cot_ref[...], conv_ref[1])
        + jnp.where(place > 0, rows_by_rows(behind_ref[...], conv_ref[2]), 0.0)
    )


def gelu_pieces(wide):
    normal_cdf = 0.5 * (1.0 + lax.erf(wide * (1.0 / math.sqrt(2.0))))
    density = jnp.exp(-0.5 * wide * wide) * (1.0 / math.sqrt(2.0 * math.pi))
    return (wide * normal_cdf, normal_cdf + wide * density)


def middle_body(*refs):
    fars, (grad_ref, send_ref, *acts) = refs[:5], refs[5:11]
    recv_ref, proj_ref, stream_ref, cot_ref, branch_ref, att_ref, sems = refs[11:]
    arriving = [
        pltpu.make_async_copy(far, near, sems.at[i])
        for i, (far, near) in enumerate(
            zip(fars, (recv_ref, proj_ref, stream_ref, cot_ref, branch_ref))
        )
    ]
    for one in arriving:
        one.start()
    ring = len(acts)
    place = lax.axis_index("seq") // (lax.axis_size("seq") // ring)
    quarter = recv_ref.shape[1] // 3
    arriving[0].wait()
    for h in range(HEADS):
        for j in range(3):
            piece = recv_ref[h, j * quarter : (j + 1) * quarter, :].astype(F32)
            at = h * VAL + j * 64
            att_ref[:, at : at + 64] = on_top(piece, 4).astype(BF)
    for one in arriving[1:]:
        one.wait()
    inside = stream_ref[...].astype(F32) + plain(att_ref[...], proj_ref[...])
    activated, slope = gelu_pieces(inside.astype(BF).astype(F32))
    grad = (cot_ref[...].astype(F32) + slope * branch_ref[...]).astype(BF)
    grad_ref[...] = grad
    out_grad = rows_by_rows(grad, proj_ref[...])
    for h in range(HEADS):
        for j in range(3):
            at = h * VAL + j * 64
            piece = side_by_side(out_grad[:, at : at + 64], 4).astype(BF)
            send_ref[h, j * quarter : (j + 1) * quarter, :] = piece
    share = activated.shape[1] // ring
    blocks = [activated[:, k * share : (k + 1) * share].astype(BF) for k in range(ring)]
    for r, act_ref in enumerate(acts):
        block = blocks[0]
        for k in range(1, ring):
            block = jnp.where(lax.rem(place + r, ring) == k, blocks[k], block)
        act_ref[...] = block


def backward_body(*refs):
    far_recv, far_att, far_own, far_prob, far_kt, far_q, far_oth = refs[:7]
    far_own_out, far_oth_out = refs[7:9]
    recv_ref, att_ref, own_ref, prob_ref, kt_ref, q_ref, oth_ref = refs[9:16]
    own_out_ref, oth_out_ref, out_ref, grad_ref, turned_ref, sems = refs[16:]
    chips, rows, _ = oth_out_ref.shape
    mine = chips * rows
    quarter = rows // 4
    block = 512
    tiles = key_tiles(own_ref, oth_ref)
    tile = 2 * mine // len(tiles)
    heres = [slice(j * tile, (j + 1) * tile) for j in range(len(tiles))]
    recv, att, own, kt, query, oth = [
        pltpu.make_async_copy(far, near, sems.at[i])
        for i, (far, near) in enumerate(
            (
                (far_recv, recv_ref),
                (far_att, att_ref),
                (far_own, own_ref),
                (far_kt, kt_ref),
                (far_q, q_ref),
                (far_oth, oth_ref),
            )
        )
    ]
    probs = [
        pltpu.make_async_copy(far_prob.at[here], prob_ref.at[here], sems.at[6 + j])
        for j, here in enumerate(heres)
    ]
    leaving = []
    for j, (side, first, step, _) in enumerate(tiles):
        if side == 1:
            at = slice(first, first + step)
            leaving.append(
                pltpu.make_async_copy(oth_out_ref.at[at], far_oth_out.at[at], sems.at[8 + j])
            )
    leaving.append(pltpu.make_async_copy(own_out_ref, far_own_out, sems.at[12]))
    order = [2, 3, 0, 1]
    for one in (recv, att, oth, probs[2], query, kt, probs[3], own, probs[0], probs[1]):
        one.start()
    recv.wait()
    for c in range(chips):
        pieces = [
            on_top(recv_ref[c, j * quarter : (j + 1) * quarter, :].astype(F32), 4) for j in range(3)
        ]
        padded = jnp.concatenate([*pieces, jnp.zeros((rows, KEY), F32)], axis=1)
        out_ref[c * rows : (c + 1) * rows, :] = padded.astype(BF)
    att.wait()
    deltas = []
    for b in range(mine // block):
        at = slice(b * block, (b + 1) * block)
        each = out_ref[at, :].astype(F32) * att_ref[at, :].astype(F32)
        delta = jnp.sum(each, axis=1, keepdims=True)
        deltas.append(jnp.transpose(jnp.broadcast_to(delta, (block, 128)))[:1, :])

    def score_grads(j):
        probs[j].wait()
        keys = tiles[j][3]()
        for b, delta in enumerate(deltas):
            at = slice(b * block, (b + 1) * block)
            grads = rows_by_rows(keys, out_ref[at, :]) - delta
            grad_ref[j % 2, :, at] = (prob_ref[heres[j], at].astype(F32) * grads).astype(BF)

    oth.wait()
    score_grads(order[0])
    query.wait()
    kt.wait()
    for i, j in enumerate(order):
        side, first, step, _ = tiles[j]
        if i + 1 < len(order):
            if i + 1 == len(order) // 2:
                own.wait()
            score_grads(order[i + 1])
        slot = grad_ref[j % 2]
        summed = plain(prob_ref[heres[j], :], out_ref[...]) + plain(slot, q_ref[...])
        near = (own_out_ref, oth_out_ref)[side]
        near[first : first + step, :rows, :] = summed.astype(BF).reshape(step, rows, WIDE)
        if side == 1:
            leaving[i].start()
        turned = plain(kt_ref[:, heres[j]], slot)
        turned_ref[...] = turned if i == 0 else turned_ref[...] + turned
    scale = 1.0 / math.sqrt(KEY)
    for b in range(mine // 384):
        turned = jnp.transpose(turned_ref[:, b * 384 : (b + 1) * 384]) * scale
        for i in range(384 // rows):
            part = turned[i * rows : (i + 1) * rows, 64:]
            own_out_ref[b * (384 // rows) + i, rows:, :] = side_by_side(part, 4).astype(BF)
    leaving[-1].start()
    for one in leaving:
        one.wait()


def weight_body(*refs):
    ring = 4
    acts, cots, (out_ref, act_ref, cot_ref) = refs[:ring], refs[ring : 2 * ring], refs[2 * ring :]
    index = lax.axis_index("seq")
    stride = lax.axis_size("seq") // ring
    place, here = index // stride, index % stride
    rows, share = acts[0].shape
    for r in range(ring):
        at = pl.ds(pl.multiple_of(lax.rem(place + r, ring) * rows, rows), rows)
        act_ref[at, :] = acts[r][...]
        cot_ref[at, :] = cots[r][...]
    bins = ring * rows
    act = jnp.transpose(act_ref[...].astype(F32)).astype(BF)
    terms = (
        plain(act[:, : bins - rows], cot_ref[rows:, :]),
        plain(act, cot_ref[...]),
        plain(act[:, rows:], cot_ref[: bins - rows, :]),
    )
    piece = share // 4
    parts = [
        jnp.concatenate([t[g * piece : (g + 1) * piece] for t in terms], axis=0) for g in range(4)
    ]
    order = []
    for r in range(4):
        part = parts[r]
        for g in range(1, 4):
            part = jnp.where(here == g, parts[g ^ r], part)
        order.append(part)
    out_ref[...] = jnp.transpose(jnp.concatenate(order, axis=0)).astype(BF)


def sum_of(refs):
    both = refs[0][...].astype(F32)
    for ref in refs[1:]:
        both = both + ref[...].astype(F32)
    return both


def dp_sum_body(terms_ref, *outs):
    both = sum_of([terms_ref.at[i] for i in range(terms_ref.shape[0])])
    width = outs[0].shape[1]
    for r, out_ref in enumerate(outs):
        out_ref[...] = both[:, r * width : (r + 1) * width]


def last_sum_body(*refs):
    both = jnp.transpose(sum_of(refs[:4])) * (1.0 / lax.axis_size("dp"))
    rows = both.shape[0] // 3
    for t in range(3):
        refs[4][t] = both[t * rows : (t + 1) * rows]


def add_body(own_ref, recv_ref, out_ref):
    rows = recv_ref.shape[1]
    for c in range(own_ref.shape[0]):
        both = own_ref[c, :rows, :].astype(F32) + recv_ref[c].astype(F32)
        out_ref[c, :rows, :] = both.astype(BF)
        out_ref[c, rows:, :] = own_ref[c, rows:, :]


def finish_body(recv_ref, q_ref, k_ref, v_ref):
    rows = q_ref.shape[0]
    for h in range(HEADS):
        v_ref[:, h * VAL : (h + 1) * VAL] = recv_ref[h, :rows, :VAL]
        k_ref[:, h * KEY : (h + 1) * KEY] = recv_ref[h, :rows, VAL:]
        q_ref[:, h * KEY : (h + 1) * KEY] = on_top(recv_ref[h, rows:, :].astype(F32), 4).astype(BF)


def shards(queries, key_rows, values, out_proj, stream, cotangent, conv_weight):
    count = lax.axis_size("seq")
    chips = count // 2
    rows = queries.shape[1]
    channels = cotangent.shape[2]
    mine = chips * rows
    same_core = [[2 * c + p for c in range(chips)] for p in range(2)]
    partner = [(i, i ^ 1) for i in range(count)]

    def shape(*dims, dtype=BF):
        return jax.ShapeDtypeStruct(dims, dtype)

    def exchange(value):
        return lax.all_to_all(value, "seq", 0, 0, axis_index_groups=same_core, tiled=True)

    def swap(value, bit=1):
        return lax.ppermute(value, "seq", [(i, i ^ bit) for i in range(count)])

    def round_ring(value, by):
        return lax.ppermute(value, "seq", [(i, (i - by) % count) for i in range(count)])

    ring = 4
    stride = count // ring
    copies = lax.axis_size("dp")
    block = 512
    pairs_done = mine * 2 * mine
    part, quarter = 3 * channels // count, rows // 4

    packed = call(pack_body, [shape(chips, rows + quarter, WIDE)], [], 60, 0, 2 * MIB, 0, "pack")(
        queries[0], key_rows[0], values[0]
    )
    own, cot = lax.optimization_barrier((exchange(packed), cotangent[0]))
    oth = swap(own)
    cots = [round_ring(cot, by * stride) for by in (1, 2, 3)]
    query, attended, lse, send = call(
        forward_body,
        [
            shape(mine, WIDE),
            shape(mine, WIDE),
            shape(mine // block, 8, block, dtype=F32),
            shape(chips, 3 * quarter, WIDE),
        ],
        [pltpu.VMEM((block, 2 * mine), F32)] * 2,
        56,
        4 * pairs_done * WIDE,
        6 * MIB,
        pairs_done,
        "forward",
    )(own, oth)
    send, *cots = lax.optimization_barrier((send, *cots))
    recv = exchange(send)
    probs, keys_turned = call(
        probs_body,
        [shape(2 * mine, mine), shape(128, 2 * mine)],
        [pltpu.VMEM((2 * mine, mine), BF), pltpu.SemaphoreType.DMA((4,))],
        56,
        2 * pairs_done * WIDE,
        12 * MIB,
        pairs_done,
        "probs",
        far_out=(0,),
    )(own, oth, query, lse)
    branch = call(
        branch_body,
        [shape(rows, channels, dtype=F32)],
        [],
        56,
        6 * rows * channels * channels,
        5 * MIB,
        0,
        "branch",
    )(cot, cots[0], cots[2], conv_weight)
    recv, probs, branch = lax.optimization_barrier((recv, probs, branch))
    ins = (recv, out_proj, stream[0], cot, branch)
    stream_grad, send, *acts = call(
        middle_body,
        [
            shape(rows, channels),
            shape(chips, 3 * quarter, WIDE),
            *[shape(rows, channels // ring)] * ring,
        ],
        [
            *[pltpu.VMEM(one.shape, one.dtype) for one in ins],
            pltpu.VMEM((rows, HEADS * VAL), BF),
            pltpu.SemaphoreType.DMA((5,)),
        ],
        56,
        4 * rows * channels * HEADS * VAL,
        5 * MIB,
        2 * rows * channels,
        "middle",
        far_in=range(5),
    )(*ins)
    recv = exchange(send)
    moved = [round_ring(acts[ring - by], by * stride) for by in (1, 2, 3)]
    terms = call(
        weight_body,
        [shape(channels, ring * part)],
        [
            pltpu.VMEM((ring * rows, channels // ring), BF),
            pltpu.VMEM((ring * rows, channels), BF),
        ],
        56,
        6 * ring * rows * channels * channels // ring,
        5 * MIB,
        0,
        "weight",
    )(acts[0], *moved, cot, *cots)
    recv, terms = lax.optimization_barrier((recv, terms))
    terms = terms.reshape(copies, channels // copies, ring * part)
    terms = lax.all_to_all(terms, "dp", 0, 0, tiled=True)
    ins = (recv, attended, own, probs, keys_turned, query, oth)
    own_grad, oth_grad = call(
        backward_body,
        [shape(chips, rows + quarter, WIDE), shape(chips, rows, WIDE)],
        [
            *[pltpu.VMEM(one.shape, one.dtype) for one in ins],
            pltpu.VMEM((chips, rows + quarter, WIDE), BF),
            pltpu.VMEM((chips, rows, WIDE), BF),
            pltpu.VMEM((mine, WIDE), BF),
            pltpu.VMEM((2, mine // 2, mine), BF),
            pltpu.VMEM((128, mine), F32),
            pltpu.SemaphoreType.DMA((13,)),
        ],
        56,
        8 * pairs_done * WIDE,
        16 * MIB,
        0,
        "backward",
        far_in=range(7),
        far_out=(0, 1),
    )(*ins)
    swapped = swap(oth_grad)
    packed = call(add_body, [shape(chips, rows + quarter, WIDE)], [], 12, 0, 3 * MIB, 0, "add")(
        own_grad, swapped
    )
    packed, terms = lax.optimization_barrier((packed, terms))
    recv = exchange(packed)
    parts = call(
        dp_sum_body,
        [shape(channels // copies, part, dtype=F32)] * ring,
        [],
        12,
        0,
        MIB,
        0,
        "dp_sum",
    )(terms)
    parts = [parts[0]] + [swap(parts[r], r) for r in (1, 2, 3)]
    weight_grad = call(
        last_sum_body,
        [shape(3, channels // count, channels // copies, dtype=F32)],
        [],
        12,
        0,
        MIB,
        0,
        "last_sum",
    )(*parts)
    query_grad, key_grad, value_grad = call(
        finish_body,
        [shape(rows, HEADS * KEY), shape(rows, HEADS * KEY), shape(rows, HEADS * VAL)],
        [],
        12,
        0,
        2 * MIB,
        0,
        "finish",
    )(recv)
    return (query_grad[None], key_grad[None], value_grad[None], stream_grad[None], weight_grad)


def solution(mesh):
    return jax.shard_map(
        shards,
        mesh=mesh,
        in_specs=(
            P("dp", "seq", None),
            P("dp", "seq", None),
            P("dp", "seq", None),
            P(),
            P("dp", "seq", None),
            P("dp", "seq", None),
            P(),
        ),
        out_specs=(
            P("dp", "seq", None),
            P("dp", "seq", None),
            P("dp", "seq", None),
            P("dp", "seq", None),
            P(None, "seq", "dp"),
        ),
        check_vma=False,
    )
```

```python
import math

import jax
import jax.numpy as jnp
from jax import lax
from jax.experimental import pallas as pl
from jax.experimental.pallas import tpu as pltpu
from jax.sharding import PartitionSpec as P

HEADS = 8
KEY = 64
VAL = 192
WIDE = VAL + KEY
LOG2E = math.log2(math.e)
BF = jnp.bfloat16
F32 = jnp.float32
MIB = 1024 * 1024


def rows_by_rows(left, right):
    return lax.dot_general(left, right, (((1,), (1,)), ((), ())), preferred_element_type=F32)


def plain(left, right):
    return lax.dot_general(left, right, (((1,), (0,)), ((), ())), preferred_element_type=F32)


def call(body, outs, scratch, vmem_mib, flops, nbytes, exps, name, far_in=(), far_out=()):
    vmem = pl.BlockSpec(memory_space=pltpu.VMEM)
    far = pl.BlockSpec(memory_space=pl.ANY)
    outs = tuple(outs)

    def run(*arrays):
        got = pl.pallas_call(
            body,
            out_shape=outs,
            in_specs=[far if i in far_in else vmem for i in range(len(arrays))],
            out_specs=tuple(far if i in far_out else vmem for i in range(len(outs))),
            scratch_shapes=list(scratch),
            compiler_params=pltpu.CompilerParams(vmem_limit_bytes=vmem_mib * MIB),
            cost_estimate=pl.CostEstimate(flops=flops, bytes_accessed=nbytes, transcendentals=exps),
            name=name,
        )(*arrays)
        return got if len(outs) > 1 else got[0]

    return run


def side_by_side(block, parts):
    rows = block.shape[0] // parts
    return jnp.concatenate([block[i * rows : (i + 1) * rows] for i in range(parts)], axis=1)


def on_top(block, parts):
    width = block.shape[1] // parts
    return jnp.concatenate([block[:, i * width : (i + 1) * width] for i in range(parts)], axis=0)


def pack_body(q_ref, k_ref, v_ref, out_ref):
    rows = q_ref.shape[0]
    for h in range(HEADS):
        out_ref[h, :rows, :VAL] = v_ref[:, h * VAL : (h + 1) * VAL]
        out_ref[h, :rows, VAL:] = k_ref[:, h * KEY : (h + 1) * KEY]
        part = q_ref[:, h * KEY : (h + 1) * KEY].astype(F32) * (1.0 / math.sqrt(KEY))
        out_ref[h, rows:, :] = side_by_side(part, 4).astype(BF)


def key_tiles(own_ref, oth_ref, count=2):
    chips = own_ref.shape[0]
    rows, step = own_ref.shape[1] * 4 // 5, chips // count
    return [
        (
            side,
            t * step,
            step,
            lambda r=ref, t=t: r[t * step : (t + 1) * step, :rows, :].reshape(step * rows, WIDE),
        )
        for side, ref in enumerate((own_ref, oth_ref))
        for t in range(count)
    ]


def forward_body(own_ref, oth_ref, q_ref, att_ref, lse_ref, send_ref, *score_refs):
    block = score_refs[0].shape[0]
    chips = own_ref.shape[0]
    rows = own_ref.shape[1] * 4 // 5
    mine = chips * rows
    blocks = mine // block
    for c in range(chips):
        query = on_top(own_ref[c, rows:, :].astype(F32), 4)
        padded = jnp.concatenate([jnp.zeros((rows, VAL), F32), query], axis=1)
        q_ref[c * rows : (c + 1) * rows, :] = padded.astype(BF)
    tiles = key_tiles(own_ref, oth_ref)
    tile = 2 * mine // len(tiles)

    def score(b, j, top):
        scores = rows_by_rows(q_ref[b * block : (b + 1) * block, :], tiles[j][3]())
        score_refs[b % 2][:, j * tile : (j + 1) * tile] = scores
        high = jnp.max(scores, axis=1, keepdims=True)
        return high if top is None else jnp.maximum(top, high)

    top = None
    for j in range(len(tiles)):
        top = score(0, j, top)
    for b in range(blocks):
        following = None
        top = top * LOG2E
        total = jnp.zeros((block, 1), F32)
        summed = jnp.zeros((block, WIDE), F32)
        for j, (_, _, _, part) in enumerate(tiles):
            if b + 1 < blocks:
                following = score(b + 1, j, following)
            expo = jnp.exp2(score_refs[b % 2][:, j * tile : (j + 1) * tile] * LOG2E - top)
            total = total + jnp.sum(expo, axis=1, keepdims=True)
            summed = summed + plain(expo.astype(BF), part())
        att_ref[b * block : (b + 1) * block, :] = (summed * (1.0 / total)).astype(BF)
        turned = jnp.transpose(jnp.broadcast_to(top + jnp.log2(total), (block, 128)))
        lse_ref[b] = turned[:8, :]
        top = following
    for c in range(chips):
        part = att_ref[c * rows : (c + 1) * rows, :].astype(F32)
        for j in range(3):
            piece = side_by_side(part[:, j * 64 : (j + 1) * 64], 4).astype(BF)
            send_ref[c, j * (rows // 4) : (j + 1) * (rows // 4), :] = piece


def probs_body(own_ref, oth_ref, q_ref, lse_ref, far_prob_ref, kt_ref, prob_ref, sems):
    blocks, _, block = lse_ref.shape
    tiles = key_tiles(own_ref, oth_ref)
    tile = prob_ref.shape[0] // len(tiles)
    for j, (_, _, _, part) in enumerate(tiles):
        here = slice(j * tile, (j + 1) * tile)
        keys = part()
        kt_ref[:, here] = jnp.transpose(keys[:, 128:].astype(F32)).astype(BF)
        for b in range(blocks):
            at = slice(b * block, (b + 1) * block)
            scores = rows_by_rows(keys, q_ref[at, :])
            prob_ref[here, at] = jnp.exp2(scores * LOG2E - lse_ref[b][:1, :]).astype(BF)
        pltpu.make_async_copy(prob_ref.at[here], far_prob_ref.at[here], sems.at[j]).start()
    for j in range(len(tiles)):
        here = slice(j * tile, (j + 1) * tile)
        pltpu.make_async_copy(prob_ref.at[here], far_prob_ref.at[here], sems.at[j]).wait()


def branch_body(cot_ref, ahead_ref, behind_ref, conv_ref, out_ref):
    ring = 4
    place = lax.axis_index("seq") // (lax.axis_size("seq") // ring)
    out_ref[...] = (
        jnp.where(place < ring - 1, rows_by_rows(ahead_ref[...], conv_ref[0]), 0.0)
        + rows_by_rows(cot_ref[...], conv_ref[1])
        + jnp.where(place > 0, rows_by_rows(behind_ref[...], conv_ref[2]), 0.0)
    )


def gelu_pieces(wide):
    normal_cdf = 0.5 * (1.0 + lax.erf(wide * (1.0 / math.sqrt(2.0))))
    density = jnp.exp(-0.5 * wide * wide) * (1.0 / math.sqrt(2.0 * math.pi))
    return (wide * normal_cdf, normal_cdf + wide * density)


def middle_body(*refs):
    fars, (grad_ref, send_ref, *acts) = refs[:5], refs[5:11]
    recv_ref, proj_ref, stream_ref, cot_ref, branch_ref, att_ref, sems = refs[11:]
    arriving = [
        pltpu.make_async_copy(far, near, sems.at[i])
        for i, (far, near) in enumerate(
            zip(fars, (recv_ref, proj_ref, stream_ref, cot_ref, branch_ref))
        )
    ]
    for one in arriving:
        one.start()
    ring = len(acts)
    place = lax.axis_index("seq") // (lax.axis_size("seq") // ring)
    quarter = recv_ref.shape[1] // 3
    arriving[0].wait()
    for h in range(HEADS):
        for j in range(3):
            piece = recv_ref[h, j * quarter : (j + 1) * quarter, :].astype(F32)
            at = h * VAL + j * 64
            att_ref[:, at : at + 64] = on_top(piece, 4).astype(BF)
    for one in arriving[1:]:
        one.wait()
    inside = stream_ref[...].astype(F32) + plain(att_ref[...], proj_ref[...])
    activated, slope = gelu_pieces(inside.astype(BF).astype(F32))
    grad = (cot_ref[...].astype(F32) + slope * branch_ref[...]).astype(BF)
    grad_ref[...] = grad
    out_grad = rows_by_rows(grad, proj_ref[...])
    for h in range(HEADS):
        for j in range(3):
            at = h * VAL + j * 64
            piece = side_by_side(out_grad[:, at : at + 64], 4).astype(BF)
            send_ref[h, j * quarter : (j + 1) * quarter, :] = piece
    share = activated.shape[1] // ring
    blocks = [activated[:, k * share : (k + 1) * share].astype(BF) for k in range(ring)]
    for r, act_ref in enumerate(acts):
        block = blocks[0]
        for k in range(1, ring):
            block = jnp.where(lax.rem(place + r, ring) == k, blocks[k], block)
        act_ref[...] = block


def backward_body(*refs):
    far_recv, far_att, far_own, far_prob, far_kt, far_q, far_oth = refs[:7]
    far_own_out, far_oth_out = refs[7:9]
    recv_ref, att_ref, own_ref, prob_ref, kt_ref, q_ref, oth_ref = refs[9:16]
    own_out_ref, oth_out_ref, out_ref, grad_ref, turned_ref, sems = refs[16:]
    chips, rows, _ = oth_out_ref.shape
    mine = chips * rows
    quarter = rows // 4
    block = 512
    tiles = key_tiles(own_ref, oth_ref)
    tile = 2 * mine // len(tiles)
    heres = [slice(j * tile, (j + 1) * tile) for j in range(len(tiles))]
    recv, att, own, kt, query, oth = [
        pltpu.make_async_copy(far, near, sems.at[i])
        for i, (far, near) in enumerate(
            (
                (far_recv, recv_ref),
                (far_att, att_ref),
                (far_own, own_ref),
                (far_kt, kt_ref),
                (far_q, q_ref),
                (far_oth, oth_ref),
            )
        )
    ]
    probs = [
        pltpu.make_async_copy(far_prob.at[here], prob_ref.at[here], sems.at[6 + j])
        for j, here in enumerate(heres)
    ]
    leaving = []
    for j, (side, first, step, _) in enumerate(tiles):
        if side == 1:
            at = slice(first, first + step)
            leaving.append(
                pltpu.make_async_copy(oth_out_ref.at[at], far_oth_out.at[at], sems.at[8 + j])
            )
    leaving.append(pltpu.make_async_copy(own_out_ref, far_own_out, sems.at[12]))
    order = [2, 3, 0, 1]
    for one in (recv, att, oth, probs[2], query, kt, probs[3], own, probs[0], probs[1]):
        one.start()
    recv.wait()
    for c in range(chips):
        pieces = [
            on_top(recv_ref[c, j * quarter : (j + 1) * quarter, :].astype(F32), 4) for j in range(3)
        ]
        padded = jnp.concatenate([*pieces, jnp.zeros((rows, KEY), F32)], axis=1)
        out_ref[c * rows : (c + 1) * rows, :] = padded.astype(BF)
    att.wait()
    deltas = []
    for b in range(mine // block):
        at = slice(b * block, (b + 1) * block)
        each = out_ref[at, :].astype(F32) * att_ref[at, :].astype(F32)
        delta = jnp.sum(each, axis=1, keepdims=True)
        deltas.append(jnp.transpose(jnp.broadcast_to(delta, (block, 128)))[:1, :])

    def score_grads(j):
        probs[j].wait()
        keys = tiles[j][3]()
        for b, delta in enumerate(deltas):
            at = slice(b * block, (b + 1) * block)
            grads = rows_by_rows(keys, out_ref[at, :]) - delta
            grad_ref[j % 2, :, at] = (prob_ref[heres[j], at].astype(F32) * grads).astype(BF)

    oth.wait()
    score_grads(order[0])
    query.wait()
    kt.wait()
    for i, j in enumerate(order):
        side, first, step, _ = tiles[j]
        if i + 1 < len(order):
            if i + 1 == len(order) // 2:
                own.wait()
            score_grads(order[i + 1])
        slot = grad_ref[j % 2]
        summed = plain(prob_ref[heres[j], :], out_ref[...]) + plain(slot, q_ref[...])
        near = (own_out_ref, oth_out_ref)[side]
        near[first : first + step, :rows, :] = summed.astype(BF).reshape(step, rows, WIDE)
        if side == 1:
            leaving[i].start()
        turned = plain(kt_ref[:, heres[j]], slot)
        turned_ref[...] = turned if i == 0 else turned_ref[...] + turned
    scale = 1.0 / math.sqrt(KEY)
    for b in range(mine // 384):
        turned = jnp.transpose(turned_ref[:, b * 384 : (b + 1) * 384]) * scale
        for i in range(384 // rows):
            part = turned[i * rows : (i + 1) * rows, 64:]
            own_out_ref[b * (384 // rows) + i, rows:, :] = side_by_side(part, 4).astype(BF)
    leaving[-1].start()
    for one in leaving:
        one.wait()


def weight_body(*refs):
    ring = 4
    acts, cots, (out_ref, act_ref, cot_ref) = refs[:ring], refs[ring : 2 * ring], refs[2 * ring :]
    index = lax.axis_index("seq")
    stride = lax.axis_size("seq") // ring
    place, here = index // stride, index % stride
    rows, share = acts[0].shape
    for r in range(ring):
        at = pl.ds(pl.multiple_of(lax.rem(place + r, ring) * rows, rows), rows)
        act_ref[at, :] = acts[r][...]
        cot_ref[at, :] = cots[r][...]
    bins = ring * rows
    act = jnp.transpose(act_ref[...].astype(F32)).astype(BF)
    terms = (
        plain(act[:, : bins - rows], cot_ref[rows:, :]),
        plain(act, cot_ref[...]),
        plain(act[:, rows:], cot_ref[: bins - rows, :]),
    )
    piece = share // 4
    parts = [
        jnp.concatenate([t[g * piece : (g + 1) * piece] for t in terms], axis=0) for g in range(4)
    ]
    order = []
    for r in range(4):
        part = parts[r]
        for g in range(1, 4):
            part = jnp.where(here == g, parts[g ^ r], part)
        order.append(part)
    out_ref[...] = jnp.transpose(jnp.concatenate(order, axis=0)).astype(BF)


def sum_of(refs):
    both = refs[0][...].astype(F32)
    for ref in refs[1:]:
        both = both + ref[...].astype(F32)
    return both


def column_sum_body(terms_ref, keep_ref, give_ref, both_ref):
    both_ref[...] = sum_of([terms_ref.at[i] for i in range(terms_ref.shape[0])])
    rows = keep_ref.shape[0]
    side = lax.axis_index("dp") % 2
    keep_ref[...] = both_ref[pl.ds(pl.multiple_of(side * rows, rows), rows), :]
    give_ref[...] = both_ref[pl.ds(pl.multiple_of((1 - side) * rows, rows), rows), :].astype(BF)


def side_sum_body(keep_ref, came_ref, *outs):
    both = sum_of((keep_ref, came_ref))
    width = outs[0].shape[1]
    for r, out_ref in enumerate(outs):
        out_ref[...] = both[:, r * width : (r + 1) * width]


def last_sum_body(*refs):
    both = jnp.transpose(sum_of(refs[:4])) * (1.0 / lax.axis_size("dp"))
    rows = both.shape[0] // 3
    for t in range(3):
        refs[4][t] = both[t * rows : (t + 1) * rows]


def add_body(own_ref, recv_ref, out_ref):
    rows = recv_ref.shape[1]
    for c in range(own_ref.shape[0]):
        both = own_ref[c, :rows, :].astype(F32) + recv_ref[c].astype(F32)
        out_ref[c, :rows, :] = both.astype(BF)
        out_ref[c, rows:, :] = own_ref[c, rows:, :]


def finish_body(recv_ref, q_ref, k_ref, v_ref):
    rows = q_ref.shape[0]
    for h in range(HEADS):
        v_ref[:, h * VAL : (h + 1) * VAL] = recv_ref[h, :rows, :VAL]
        k_ref[:, h * KEY : (h + 1) * KEY] = recv_ref[h, :rows, VAL:]
        q_ref[:, h * KEY : (h + 1) * KEY] = on_top(recv_ref[h, rows:, :].astype(F32), 4).astype(BF)


def shards(queries, key_rows, values, out_proj, stream, cotangent, conv_weight):
    count = lax.axis_size("seq")
    chips = count // 2
    rows = queries.shape[1]
    channels = cotangent.shape[2]
    mine = chips * rows
    same_core = [[2 * c + p for c in range(chips)] for p in range(2)]
    partner = [(i, i ^ 1) for i in range(count)]

    def shape(*dims, dtype=BF):
        return jax.ShapeDtypeStruct(dims, dtype)

    def exchange(value):
        return lax.all_to_all(value, "seq", 0, 0, axis_index_groups=same_core, tiled=True)

    def swap(value, bit=1):
        return lax.ppermute(value, "seq", [(i, i ^ bit) for i in range(count)])

    def round_ring(value, by):
        return lax.ppermute(value, "seq", [(i, (i - by) % count) for i in range(count)])

    ring = 4
    stride = count // ring
    copies = lax.axis_size("dp")
    block = 512
    pairs_done = mine * 2 * mine
    part, quarter = 3 * channels // count, rows // 4

    packed = call(pack_body, [shape(chips, rows + quarter, WIDE)], [], 60, 0, 2 * MIB, 0, "pack")(
        queries[0], key_rows[0], values[0]
    )
    own, cot = lax.optimization_barrier((exchange(packed), cotangent[0]))
    oth = swap(own)
    ahead, behind = round_ring(cot, stride), round_ring(cot, 3 * stride)
    query, attended, lse, send = call(
        forward_body,
        [
            shape(mine, WIDE),
            shape(mine, WIDE),
            shape(mine // block, 8, block, dtype=F32),
            shape(chips, 3 * quarter, WIDE),
        ],
        [pltpu.VMEM((block, 2 * mine), F32)] * 2,
        56,
        4 * pairs_done * WIDE,
        6 * MIB,
        pairs_done,
        "forward",
    )(own, oth)
    send, ahead, behind = lax.optimization_barrier((send, ahead, behind))
    recv = exchange(send)
    across = round_ring(ahead, stride)
    probs, keys_turned = call(
        probs_body,
        [shape(2 * mine, mine), shape(128, 2 * mine)],
        [pltpu.VMEM((2 * mine, mine), BF), pltpu.SemaphoreType.DMA((4,))],
        56,
        2 * pairs_done * WIDE,
        12 * MIB,
        pairs_done,
        "probs",
        far_out=(0,),
    )(own, oth, query, lse)
    branch = call(
        branch_body,
        [shape(rows, channels, dtype=F32)],
        [],
        56,
        6 * rows * channels * channels,
        5 * MIB,
        0,
        "branch",
    )(cot, ahead, behind, conv_weight)
    recv, branch, across = lax.optimization_barrier((recv, branch, across))
    ins = (recv, out_proj, stream[0], cot, branch)
    stream_grad, send, *acts = call(
        middle_body,
        [
            shape(rows, channels),
            shape(chips, 3 * quarter, WIDE),
            *[shape(rows, channels // ring)] * ring,
        ],
        [
            *[pltpu.VMEM(one.shape, one.dtype) for one in ins],
            pltpu.VMEM((rows, HEADS * VAL), BF),
            pltpu.SemaphoreType.DMA((5,)),
        ],
        56,
        4 * rows * channels * HEADS * VAL,
        5 * MIB,
        2 * rows * channels,
        "middle",
        far_in=range(5),
    )(*ins)
    recv = exchange(send)
    moved = [round_ring(acts[ring - by], by * stride) for by in (1, 2, 3)]
    terms = call(
        weight_body,
        [shape(channels, ring * part)],
        [
            pltpu.VMEM((ring * rows, channels // ring), BF),
            pltpu.VMEM((ring * rows, channels), BF),
        ],
        56,
        6 * ring * rows * channels * channels // ring,
        5 * MIB,
        0,
        "weight",
    )(acts[0], *moved, cot, ahead, across, behind)
    recv, terms, probs, keys_turned = lax.optimization_barrier((recv, terms, probs, keys_turned))
    layers = copies // 2
    terms = terms.reshape(layers, channels // layers, ring * part)
    columns = [[2 * z + y for z in range(layers)] for y in range(2)]
    terms = lax.all_to_all(terms, "dp", 0, 0, axis_index_groups=columns, tiled=True)
    ins = (recv, attended, own, probs, keys_turned, query, oth)
    own_grad, oth_grad = call(
        backward_body,
        [shape(chips, rows + quarter, WIDE), shape(chips, rows, WIDE)],
        [
            *[pltpu.VMEM(one.shape, one.dtype) for one in ins],
            pltpu.VMEM((chips, rows + quarter, WIDE), BF),
            pltpu.VMEM((chips, rows, WIDE), BF),
            pltpu.VMEM((mine, WIDE), BF),
            pltpu.VMEM((2, mine // 2, mine), BF),
            pltpu.VMEM((128, mine), F32),
            pltpu.SemaphoreType.DMA((13,)),
        ],
        56,
        8 * pairs_done * WIDE,
        16 * MIB,
        0,
        "backward",
        far_in=range(7),
        far_out=(0, 1),
    )(*ins)
    terms, oth_grad = lax.optimization_barrier((terms, oth_grad))
    swapped = swap(oth_grad)
    share = channels // copies
    keep, give = call(
        column_sum_body,
        [shape(share, ring * part, dtype=F32), shape(share, ring * part)],
        [pltpu.VMEM((2 * share, ring * part), F32)],
        12,
        0,
        MIB,
        0,
        "column_sum",
    )(terms)
    came = lax.ppermute(give, "dp", [(i, i ^ 1) for i in range(copies)])
    packed = call(add_body, [shape(chips, rows + quarter, WIDE)], [], 12, 0, 3 * MIB, 0, "add")(
        own_grad, swapped
    )
    packed, came = lax.optimization_barrier((packed, came))
    recv = exchange(packed)
    parts = call(
        side_sum_body, [shape(share, part, dtype=F32)] * ring, [], 12, 0, MIB, 0, "side_sum"
    )(keep, came)
    parts = [parts[0]] + [swap(parts[r], r) for r in (1, 2, 3)]
    weight_grad = call(
        last_sum_body,
        [shape(3, channels // count, channels // copies, dtype=F32)],
        [],
        12,
        0,
        MIB,
        0,
        "last_sum",
    )(*parts)
    query_grad, key_grad, value_grad = call(
        finish_body,
        [shape(rows, HEADS * KEY), shape(rows, HEADS * KEY), shape(rows, HEADS * VAL)],
        [],
        12,
        0,
        2 * MIB,
        0,
        "finish",
    )(recv)
    return (query_grad[None], key_grad[None], value_grad[None], stream_grad[None], weight_grad)


def solution(mesh):
    return jax.shard_map(
        shards,
        mesh=mesh,
        in_specs=(
            P("dp", "seq", None),
            P("dp", "seq", None),
            P("dp", "seq", None),
            P(),
            P("dp", "seq", None),
            P("dp", "seq", None),
            P(),
        ),
        out_specs=(
            P("dp", "seq", None),
            P("dp", "seq", None),
            P("dp", "seq", None),
            P("dp", "seq", None),
            P(None, "seq", "dp"),
        ),
        check_vma=False,
    )
```

```python
import math

import jax
import jax.numpy as jnp
from jax import lax
from jax.experimental import pallas as pl
from jax.experimental.pallas import tpu as pltpu
from jax.sharding import PartitionSpec as P

HEADS = 8
KEY = 64
VAL = 192
WIDE = VAL + KEY
LOG2E = math.log2(math.e)
BF = jnp.bfloat16
F32 = jnp.float32
MIB = 1024 * 1024


def rows_by_rows(left, right):
    return lax.dot_general(left, right, (((1,), (1,)), ((), ())), preferred_element_type=F32)


def plain(left, right):
    return lax.dot_general(left, right, (((1,), (0,)), ((), ())), preferred_element_type=F32)


def call(body, outs, scratch, vmem_mib, flops, nbytes, exps, name, far_in=(), far_out=()):
    vmem = pl.BlockSpec(memory_space=pltpu.VMEM)
    far = pl.BlockSpec(memory_space=pl.ANY)
    outs = tuple(outs)

    def run(*arrays):
        got = pl.pallas_call(
            body,
            out_shape=outs,
            in_specs=[far if i in far_in else vmem for i in range(len(arrays))],
            out_specs=tuple(far if i in far_out else vmem for i in range(len(outs))),
            scratch_shapes=list(scratch),
            compiler_params=pltpu.CompilerParams(vmem_limit_bytes=vmem_mib * MIB),
            cost_estimate=pl.CostEstimate(flops=flops, bytes_accessed=nbytes, transcendentals=exps),
            name=name,
        )(*arrays)
        return got if len(outs) > 1 else got[0]

    return run


def side_by_side(block, parts):
    rows = block.shape[0] // parts
    return jnp.concatenate([block[i * rows : (i + 1) * rows] for i in range(parts)], axis=1)


def on_top(block, parts):
    width = block.shape[1] // parts
    return jnp.concatenate([block[:, i * width : (i + 1) * width] for i in range(parts)], axis=0)


def pack_body(q_ref, k_ref, v_ref, out_ref):
    rows = q_ref.shape[0]
    for h in range(HEADS):
        out_ref[h, :rows, :VAL] = v_ref[:, h * VAL : (h + 1) * VAL]
        out_ref[h, :rows, VAL:] = k_ref[:, h * KEY : (h + 1) * KEY]
        part = q_ref[:, h * KEY : (h + 1) * KEY].astype(F32) * (1.0 / math.sqrt(KEY))
        out_ref[h, rows:, :] = side_by_side(part, 4).astype(BF)


def key_tiles(own_ref, oth_ref, count=2):
    chips = own_ref.shape[0]
    rows, step = own_ref.shape[1] * 4 // 5, chips // count
    return [
        (
            side,
            t * step,
            step,
            lambda r=ref, t=t: r[t * step : (t + 1) * step, :rows, :].reshape(step * rows, WIDE),
        )
        for side, ref in enumerate((own_ref, oth_ref))
        for t in range(count)
    ]


def forward_body(own_ref, oth_ref, q_ref, att_ref, lse_ref, send_ref, *score_refs):
    block = score_refs[0].shape[0]
    chips = own_ref.shape[0]
    rows = own_ref.shape[1] * 4 // 5
    mine = chips * rows
    blocks = mine // block
    for c in range(chips):
        query = on_top(own_ref[c, rows:, :].astype(F32), 4)
        padded = jnp.concatenate([jnp.zeros((rows, VAL), F32), query], axis=1)
        q_ref[c * rows : (c + 1) * rows, :] = padded.astype(BF)
    tiles = key_tiles(own_ref, oth_ref)
    tile = 2 * mine // len(tiles)

    def score(b, j, top):
        scores = rows_by_rows(q_ref[b * block : (b + 1) * block, :], tiles[j][3]())
        score_refs[b % 2][:, j * tile : (j + 1) * tile] = scores
        high = jnp.max(scores, axis=1, keepdims=True)
        return high if top is None else jnp.maximum(top, high)

    top = None
    for j in range(len(tiles)):
        top = score(0, j, top)
    for b in range(blocks):
        following = None
        top = top * LOG2E
        total = jnp.zeros((block, 1), F32)
        summed = jnp.zeros((block, WIDE), F32)
        for j, (_, _, _, part) in enumerate(tiles):
            if b + 1 < blocks:
                following = score(b + 1, j, following)
            expo = jnp.exp2(score_refs[b % 2][:, j * tile : (j + 1) * tile] * LOG2E - top)
            total = total + jnp.sum(expo, axis=1, keepdims=True)
            summed = summed + plain(expo.astype(BF), part())
        att_ref[b * block : (b + 1) * block, :] = (summed * (1.0 / total)).astype(BF)
        turned = jnp.transpose(jnp.broadcast_to(top + jnp.log2(total), (block, 128)))
        lse_ref[b] = turned[:8, :]
        top = following
    for c in range(chips):
        part = att_ref[c * rows : (c + 1) * rows, :].astype(F32)
        for j in range(3):
            piece = side_by_side(part[:, j * 64 : (j + 1) * 64], 4).astype(BF)
            send_ref[c, j * (rows // 4) : (j + 1) * (rows // 4), :] = piece


def probs_body(own_ref, oth_ref, q_ref, lse_ref, far_prob_ref, kt_ref, prob_ref, sems):
    blocks, _, block = lse_ref.shape
    tiles = key_tiles(own_ref, oth_ref)
    tile = prob_ref.shape[0] // len(tiles)
    for j, (_, _, _, part) in enumerate(tiles):
        here = slice(j * tile, (j + 1) * tile)
        keys = part()
        kt_ref[:, here] = jnp.transpose(keys[:, 128:].astype(F32)).astype(BF)
        for b in range(blocks):
            at = slice(b * block, (b + 1) * block)
            scores = rows_by_rows(keys, q_ref[at, :])
            prob_ref[here, at] = jnp.exp2(scores * LOG2E - lse_ref[b][:1, :]).astype(BF)
        pltpu.make_async_copy(prob_ref.at[here], far_prob_ref.at[here], sems.at[j]).start()
    for j in range(len(tiles)):
        here = slice(j * tile, (j + 1) * tile)
        pltpu.make_async_copy(prob_ref.at[here], far_prob_ref.at[here], sems.at[j]).wait()


def branch_body(cot_ref, ahead_ref, behind_ref, conv_ref, out_ref):
    ring = 4
    place = lax.axis_index("seq") // (lax.axis_size("seq") // ring)
    out_ref[...] = (
        jnp.where(place < ring - 1, rows_by_rows(ahead_ref[...], conv_ref[0]), 0.0)
        + rows_by_rows(cot_ref[...], conv_ref[1])
        + jnp.where(place > 0, rows_by_rows(behind_ref[...], conv_ref[2]), 0.0)
    )


def gelu_pieces(wide):
    normal_cdf = 0.5 * (1.0 + lax.erf(wide * (1.0 / math.sqrt(2.0))))
    density = jnp.exp(-0.5 * wide * wide) * (1.0 / math.sqrt(2.0 * math.pi))
    return (wide * normal_cdf, normal_cdf + wide * density)


def middle_body(*refs):
    fars, (grad_ref, send_ref, *acts) = refs[:5], refs[5:11]
    recv_ref, proj_ref, stream_ref, cot_ref, branch_ref, att_ref, sems = refs[11:]
    arriving = [
        pltpu.make_async_copy(far, near, sems.at[i])
        for i, (far, near) in enumerate(
            zip(fars, (recv_ref, proj_ref, stream_ref, cot_ref, branch_ref))
        )
    ]
    for one in arriving:
        one.start()
    ring = len(acts)
    place = lax.axis_index("seq") // (lax.axis_size("seq") // ring)
    quarter = recv_ref.shape[1] // 3
    arriving[0].wait()
    for h in range(HEADS):
        for j in range(3):
            piece = recv_ref[h, j * quarter : (j + 1) * quarter, :].astype(F32)
            at = h * VAL + j * 64
            att_ref[:, at : at + 64] = on_top(piece, 4).astype(BF)
    for one in arriving[1:]:
        one.wait()
    inside = stream_ref[...].astype(F32) + plain(att_ref[...], proj_ref[...])
    activated, slope = gelu_pieces(inside.astype(BF).astype(F32))
    grad = (cot_ref[...].astype(F32) + slope * branch_ref[...]).astype(BF)
    grad_ref[...] = grad
    out_grad = rows_by_rows(grad, proj_ref[...])
    for h in range(HEADS):
        for j in range(3):
            at = h * VAL + j * 64
            piece = side_by_side(out_grad[:, at : at + 64], 4).astype(BF)
            send_ref[h, j * quarter : (j + 1) * quarter, :] = piece
    share = activated.shape[1] // ring
    blocks = [activated[:, k * share : (k + 1) * share].astype(BF) for k in range(ring)]
    for r, act_ref in enumerate(acts):
        block = blocks[0]
        for k in range(1, ring):
            block = jnp.where(lax.rem(place + r, ring) == k, blocks[k], block)
        act_ref[...] = block


def backward_body(*refs):
    far_recv, far_att, far_own, far_prob, far_kt, far_q, far_oth = refs[:7]
    far_own_out, far_oth_out = refs[7:9]
    recv_ref, att_ref, own_ref, prob_ref, kt_ref, q_ref, oth_ref = refs[9:16]
    own_out_ref, oth_out_ref, out_ref, grad_ref, turned_ref, sems = refs[16:]
    chips, rows, _ = oth_out_ref.shape
    mine = chips * rows
    quarter = rows // 4
    block = 512
    tiles = key_tiles(own_ref, oth_ref)
    tile = 2 * mine // len(tiles)
    heres = [slice(j * tile, (j + 1) * tile) for j in range(len(tiles))]
    recv, att, own, kt, query, oth = [
        pltpu.make_async_copy(far, near, sems.at[i])
        for i, (far, near) in enumerate(
            (
                (far_recv, recv_ref),
                (far_att, att_ref),
                (far_own, own_ref),
                (far_kt, kt_ref),
                (far_q, q_ref),
                (far_oth, oth_ref),
            )
        )
    ]
    probs = [
        pltpu.make_async_copy(far_prob.at[here], prob_ref.at[here], sems.at[6 + j])
        for j, here in enumerate(heres)
    ]
    leaving = []
    for j, (side, first, step, _) in enumerate(tiles):
        if side == 1:
            at = slice(first, first + step)
            leaving.append(
                pltpu.make_async_copy(oth_out_ref.at[at], far_oth_out.at[at], sems.at[8 + j])
            )
    leaving.append(pltpu.make_async_copy(own_out_ref, far_own_out, sems.at[12]))
    order = [2, 3, 0, 1]
    for one in (recv, att, oth, probs[2], query, kt, probs[3], own, probs[0], probs[1]):
        one.start()
    recv.wait()
    for c in range(chips):
        pieces = [
            on_top(recv_ref[c, j * quarter : (j + 1) * quarter, :].astype(F32), 4) for j in range(3)
        ]
        padded = jnp.concatenate([*pieces, jnp.zeros((rows, KEY), F32)], axis=1)
        out_ref[c * rows : (c + 1) * rows, :] = padded.astype(BF)
    att.wait()
    deltas = []
    for b in range(mine // block):
        at = slice(b * block, (b + 1) * block)
        each = out_ref[at, :].astype(F32) * att_ref[at, :].astype(F32)
        delta = jnp.sum(each, axis=1, keepdims=True)
        deltas.append(jnp.transpose(jnp.broadcast_to(delta, (block, 128)))[:1, :])

    def score_grads(j):
        probs[j].wait()
        keys = tiles[j][3]()
        for b, delta in enumerate(deltas):
            at = slice(b * block, (b + 1) * block)
            grads = rows_by_rows(keys, out_ref[at, :]) - delta
            grad_ref[j % 2, :, at] = (prob_ref[heres[j], at].astype(F32) * grads).astype(BF)

    oth.wait()
    score_grads(order[0])
    query.wait()
    kt.wait()
    for i, j in enumerate(order):
        side, first, step, _ = tiles[j]
        if i + 1 < len(order):
            if i + 1 == len(order) // 2:
                own.wait()
            score_grads(order[i + 1])
        slot = grad_ref[j % 2]
        summed = plain(prob_ref[heres[j], :], out_ref[...]) + plain(slot, q_ref[...])
        near = (own_out_ref, oth_out_ref)[side]
        near[first : first + step, :rows, :] = summed.astype(BF).reshape(step, rows, WIDE)
        if side == 1:
            leaving[i].start()
        turned = plain(kt_ref[:, heres[j]], slot)
        turned_ref[...] = turned if i == 0 else turned_ref[...] + turned
    scale = 1.0 / math.sqrt(KEY)
    for b in range(mine // 384):
        turned = jnp.transpose(turned_ref[:, b * 384 : (b + 1) * 384]) * scale
        for i in range(384 // rows):
            part = turned[i * rows : (i + 1) * rows, 64:]
            own_out_ref[b * (384 // rows) + i, rows:, :] = side_by_side(part, 4).astype(BF)
    leaving[-1].start()
    for one in leaving:
        one.wait()


def weight_body(*refs):
    ring = 4
    acts, cots, (out_ref, act_ref, cot_ref) = refs[:ring], refs[ring : 2 * ring], refs[2 * ring :]
    index = lax.axis_index("seq")
    stride = lax.axis_size("seq") // ring
    place, here = index // stride, index % stride
    rows, share = acts[0].shape
    for r in range(ring):
        at = pl.ds(pl.multiple_of(lax.rem(place + r, ring) * rows, rows), rows)
        act_ref[at, :] = acts[r][...]
        cot_ref[at, :] = cots[r][...]
    bins = ring * rows
    act = jnp.transpose(act_ref[...].astype(F32)).astype(BF)
    terms = (
        plain(act[:, : bins - rows], cot_ref[rows:, :]),
        plain(act, cot_ref[...]),
        plain(act[:, rows:], cot_ref[: bins - rows, :]),
    )
    piece = share // 4
    parts = [
        jnp.concatenate([t[g * piece : (g + 1) * piece] for t in terms], axis=0) for g in range(4)
    ]
    order = []
    for r in range(4):
        part = parts[r]
        for g in range(1, 4):
            part = jnp.where(here == g, parts[g ^ r], part)
        order.append(part)
    out_ref[...] = jnp.transpose(jnp.concatenate(order, axis=0)).astype(BF)


def sum_of(refs):
    both = refs[0][...].astype(F32)
    for ref in refs[1:]:
        both = both + ref[...].astype(F32)
    return both


def dp_sum_body(terms_ref, *outs):
    both = sum_of([terms_ref.at[i] for i in range(terms_ref.shape[0])])
    width = outs[0].shape[1]
    for r, out_ref in enumerate(outs):
        out_ref[...] = both[:, r * width : (r + 1) * width]


def last_sum_body(*refs):
    both = jnp.transpose(sum_of(refs[:4])) * (1.0 / lax.axis_size("dp"))
    rows = both.shape[0] // 3
    for t in range(3):
        refs[4][t] = both[t * rows : (t + 1) * rows]


def add_body(own_ref, recv_ref, out_ref):
    rows = recv_ref.shape[1]
    for c in range(own_ref.shape[0]):
        both = own_ref[c, :rows, :].astype(F32) + recv_ref[c].astype(F32)
        out_ref[c, :rows, :] = both.astype(BF)
        out_ref[c, rows:, :] = own_ref[c, rows:, :]


def finish_body(recv_ref, q_ref, k_ref, v_ref):
    rows = q_ref.shape[0]
    for h in range(HEADS):
        v_ref[:, h * VAL : (h + 1) * VAL] = recv_ref[h, :rows, :VAL]
        k_ref[:, h * KEY : (h + 1) * KEY] = recv_ref[h, :rows, VAL:]
        q_ref[:, h * KEY : (h + 1) * KEY] = on_top(recv_ref[h, rows:, :].astype(F32), 4).astype(BF)


def shards(queries, key_rows, values, out_proj, stream, cotangent, conv_weight):
    count = lax.axis_size("seq")
    chips = count // 2
    rows = queries.shape[1]
    channels = cotangent.shape[2]
    mine = chips * rows
    same_core = [[2 * c + p for c in range(chips)] for p in range(2)]
    partner = [(i, i ^ 1) for i in range(count)]

    def shape(*dims, dtype=BF):
        return jax.ShapeDtypeStruct(dims, dtype)

    def exchange(value):
        return lax.all_to_all(value, "seq", 0, 0, axis_index_groups=same_core, tiled=True)

    def swap(value, bit=1):
        return lax.ppermute(value, "seq", [(i, i ^ bit) for i in range(count)])

    def round_ring(value, by):
        return lax.ppermute(value, "seq", [(i, (i - by) % count) for i in range(count)])

    ring = 4
    stride = count // ring
    copies = lax.axis_size("dp")
    block = 512
    pairs_done = mine * 2 * mine
    part, quarter = 3 * channels // count, rows // 4

    packed = call(pack_body, [shape(chips, rows + quarter, WIDE)], [], 60, 0, 2 * MIB, 0, "pack")(
        queries[0], key_rows[0], values[0]
    )
    own, cot = lax.optimization_barrier((exchange(packed), cotangent[0]))
    oth = swap(own)
    ahead, behind = round_ring(cot, stride), round_ring(cot, 3 * stride)
    query, attended, lse, send = call(
        forward_body,
        [
            shape(mine, WIDE),
            shape(mine, WIDE),
            shape(mine // block, 8, block, dtype=F32),
            shape(chips, 3 * quarter, WIDE),
        ],
        [pltpu.VMEM((block, 2 * mine), F32)] * 2,
        56,
        4 * pairs_done * WIDE,
        6 * MIB,
        pairs_done,
        "forward",
    )(own, oth)
    send, ahead, behind = lax.optimization_barrier((send, ahead, behind))
    recv = exchange(send)
    across = round_ring(ahead, stride)
    probs, keys_turned = call(
        probs_body,
        [shape(2 * mine, mine), shape(128, 2 * mine)],
        [pltpu.VMEM((2 * mine, mine), BF), pltpu.SemaphoreType.DMA((4,))],
        56,
        2 * pairs_done * WIDE,
        12 * MIB,
        pairs_done,
        "probs",
        far_out=(0,),
    )(own, oth, query, lse)
    branch = call(
        branch_body,
        [shape(rows, channels, dtype=F32)],
        [],
        56,
        6 * rows * channels * channels,
        5 * MIB,
        0,
        "branch",
    )(cot, ahead, behind, conv_weight)
    recv, branch = lax.optimization_barrier((recv, branch))
    ins = (recv, out_proj, stream[0], cot, branch)
    stream_grad, send, *acts = call(
        middle_body,
        [
            shape(rows, channels),
            shape(chips, 3 * quarter, WIDE),
            *[shape(rows, channels // ring)] * ring,
        ],
        [
            *[pltpu.VMEM(one.shape, one.dtype) for one in ins],
            pltpu.VMEM((rows, HEADS * VAL), BF),
            pltpu.SemaphoreType.DMA((5,)),
        ],
        56,
        4 * rows * channels * HEADS * VAL,
        5 * MIB,
        2 * rows * channels,
        "middle",
        far_in=range(5),
    )(*ins)
    recv = exchange(send)
    across, *acts = lax.optimization_barrier((across, *acts))
    moved = [round_ring(acts[ring - by], by * stride) for by in (1, 2, 3)]
    terms = call(
        weight_body,
        [shape(channels, ring * part)],
        [
            pltpu.VMEM((ring * rows, channels // ring), BF),
            pltpu.VMEM((ring * rows, channels), BF),
        ],
        56,
        6 * ring * rows * channels * channels // ring,
        5 * MIB,
        0,
        "weight",
    )(acts[0], *moved, cot, ahead, across, behind)
    recv, terms, probs, keys_turned = lax.optimization_barrier((recv, terms, probs, keys_turned))
    terms = terms.reshape(copies, channels // copies, ring * part)
    terms = lax.all_to_all(terms, "dp", 0, 0, tiled=True)
    ins = (recv, attended, own, probs, keys_turned, query, oth)
    own_grad, oth_grad = call(
        backward_body,
        [shape(chips, rows + quarter, WIDE), shape(chips, rows, WIDE)],
        [
            *[pltpu.VMEM(one.shape, one.dtype) for one in ins],
            pltpu.VMEM((chips, rows + quarter, WIDE), BF),
            pltpu.VMEM((chips, rows, WIDE), BF),
            pltpu.VMEM((mine, WIDE), BF),
            pltpu.VMEM((2, mine // 2, mine), BF),
            pltpu.VMEM((128, mine), F32),
            pltpu.SemaphoreType.DMA((13,)),
        ],
        56,
        8 * pairs_done * WIDE,
        16 * MIB,
        0,
        "backward",
        far_in=range(7),
        far_out=(0, 1),
    )(*ins)
    swapped = swap(oth_grad)
    packed = call(add_body, [shape(chips, rows + quarter, WIDE)], [], 12, 0, 3 * MIB, 0, "add")(
        own_grad, swapped
    )
    packed, terms = lax.optimization_barrier((packed, terms))
    recv = exchange(packed)
    parts = call(
        dp_sum_body,
        [shape(channels // copies, part, dtype=F32)] * ring,
        [],
        12,
        0,
        MIB,
        0,
        "dp_sum",
    )(terms)
    parts = [parts[0]] + [swap(parts[r], r) for r in (1, 2, 3)]
    weight_grad = call(
        last_sum_body,
        [shape(3, channels // count, channels // copies, dtype=F32)],
        [],
        12,
        0,
        MIB,
        0,
        "last_sum",
    )(*parts)
    query_grad, key_grad, value_grad = call(
        finish_body,
        [shape(rows, HEADS * KEY), shape(rows, HEADS * KEY), shape(rows, HEADS * VAL)],
        [],
        12,
        0,
        2 * MIB,
        0,
        "finish",
    )(recv)
    return (query_grad[None], key_grad[None], value_grad[None], stream_grad[None], weight_grad)


def solution(mesh):
    return jax.shard_map(
        shards,
        mesh=mesh,
        in_specs=(
            P("dp", "seq", None),
            P("dp", "seq", None),
            P("dp", "seq", None),
            P(),
            P("dp", "seq", None),
            P("dp", "seq", None),
            P(),
        ),
        out_specs=(
            P("dp", "seq", None),
            P("dp", "seq", None),
            P("dp", "seq", None),
            P("dp", "seq", None),
            P(None, "seq", "dp"),
        ),
        check_vma=False,
    )
```

```python
import math

import jax
import jax.numpy as jnp
from jax import lax
from jax.experimental import pallas as pl
from jax.experimental.pallas import tpu as pltpu
from jax.sharding import PartitionSpec as P

HEADS = 8
KEY = 64
VAL = 192
WIDE = VAL + KEY
LOG2E = math.log2(math.e)
BF = jnp.bfloat16
F32 = jnp.float32
MIB = 1024 * 1024


def rows_by_rows(left, right):
    return lax.dot_general(left, right, (((1,), (1,)), ((), ())), preferred_element_type=F32)


def plain(left, right):
    return lax.dot_general(left, right, (((1,), (0,)), ((), ())), preferred_element_type=F32)


def call(body, outs, scratch, vmem_mib, flops, nbytes, exps, name, far_in=(), far_out=()):
    vmem = pl.BlockSpec(memory_space=pltpu.VMEM)
    far = pl.BlockSpec(memory_space=pl.ANY)
    outs = tuple(outs)

    def run(*arrays):
        got = pl.pallas_call(
            body,
            out_shape=outs,
            in_specs=[far if i in far_in else vmem for i in range(len(arrays))],
            out_specs=tuple(far if i in far_out else vmem for i in range(len(outs))),
            scratch_shapes=list(scratch),
            compiler_params=pltpu.CompilerParams(vmem_limit_bytes=vmem_mib * MIB),
            cost_estimate=pl.CostEstimate(flops=flops, bytes_accessed=nbytes, transcendentals=exps),
            name=name,
        )(*arrays)
        return got if len(outs) > 1 else got[0]

    return run


def side_by_side(block, parts):
    rows = block.shape[0] // parts
    return jnp.concatenate([block[i * rows : (i + 1) * rows] for i in range(parts)], axis=1)


def on_top(block, parts):
    width = block.shape[1] // parts
    return jnp.concatenate([block[:, i * width : (i + 1) * width] for i in range(parts)], axis=0)


def pack_body(q_ref, k_ref, far_v, far_out, v_ref, out_ref, sems):
    rows = q_ref.shape[0]
    value = pltpu.make_async_copy(far_v, v_ref, sems.at[HEADS])
    value.start()
    for h in range(HEADS):
        out_ref[h, :rows, VAL:] = k_ref[:, h * KEY : (h + 1) * KEY]
        part = q_ref[:, h * KEY : (h + 1) * KEY].astype(F32) * (1.0 / math.sqrt(KEY))
        out_ref[h, rows:, :] = side_by_side(part, 4).astype(BF)
    value.wait()
    leaving = []
    for h in range(HEADS):
        out_ref[h, :rows, :VAL] = v_ref[:, h * VAL : (h + 1) * VAL]
        leaving.append(pltpu.make_async_copy(out_ref.at[h], far_out.at[h], sems.at[h]))
        leaving[-1].start()
    for one in leaving:
        one.wait()


def key_tiles(own_ref, oth_ref, count=2):
    chips = own_ref.shape[0]
    rows, step = own_ref.shape[1] * 4 // 5, chips // count
    return [
        (
            side,
            t * step,
            step,
            lambda r=ref, t=t: r[t * step : (t + 1) * step, :rows, :].reshape(step * rows, WIDE),
        )
        for side, ref in enumerate((own_ref, oth_ref))
        for t in range(count)
    ]


def forward_body(own_ref, far_oth, far_q, far_att, lse_ref, send_ref, *rest):
    oth_ref, q_ref, att_ref, sems, *score_refs = rest
    block = score_refs[0].shape[0]
    oth = pltpu.make_async_copy(far_oth, oth_ref, sems.at[0])
    oth.start()
    chips = own_ref.shape[0]
    rows = own_ref.shape[1] * 4 // 5
    mine = chips * rows
    blocks = mine // block
    for c in range(chips):
        query = on_top(own_ref[c, rows:, :].astype(F32), 4)
        padded = jnp.concatenate([jnp.zeros((rows, VAL), F32), query], axis=1)
        q_ref[c * rows : (c + 1) * rows, :] = padded.astype(BF)
    leaving = [pltpu.make_async_copy(q_ref, far_q, sems.at[1])]
    leaving[0].start()
    tiles = key_tiles(own_ref, oth_ref)
    tile = 2 * mine // len(tiles)

    def score(b, j, top):
        scores = rows_by_rows(q_ref[b * block : (b + 1) * block, :], tiles[j][3]())
        score_refs[b % 2][:, j * tile : (j + 1) * tile] = scores
        high = jnp.max(scores, axis=1, keepdims=True)
        return high if top is None else jnp.maximum(top, high)

    top = None
    for j in range(len(tiles)):
        if j == len(tiles) // 2:
            oth.wait()
        top = score(0, j, top)
    for b in range(blocks):
        following = None
        top = top * LOG2E
        total = jnp.zeros((block, 1), F32)
        summed = jnp.zeros((block, WIDE), F32)
        for j, (_, _, _, part) in enumerate(tiles):
            if b + 1 < blocks:
                following = score(b + 1, j, following)
            expo = jnp.exp2(score_refs[b % 2][:, j * tile : (j + 1) * tile] * LOG2E - top)
            total = total + jnp.sum(expo, axis=1, keepdims=True)
            summed = summed + plain(expo.astype(BF), part())
        at = slice(b * block, (b + 1) * block)
        att_ref[at, :] = (summed * (1.0 / total)).astype(BF)
        leaving.append(pltpu.make_async_copy(att_ref.at[at], far_att.at[at], sems.at[2 + b]))
        leaving[-1].start()
        turned = jnp.transpose(jnp.broadcast_to(top + jnp.log2(total), (block, 128)))
        lse_ref[b] = turned[:8, :]
        top = following
    for c in range(chips):
        part = att_ref[c * rows : (c + 1) * rows, :].astype(F32)
        for j in range(3):
            piece = side_by_side(part[:, j * 64 : (j + 1) * 64], 4).astype(BF)
            send_ref[c, j * (rows // 4) : (j + 1) * (rows // 4), :] = piece
    for one in leaving:
        one.wait()


def probs_body(own_ref, oth_ref, q_ref, lse_ref, far_prob_ref, kt_ref, prob_ref, sems):
    blocks, _, block = lse_ref.shape
    tiles = key_tiles(own_ref, oth_ref)
    tile = prob_ref.shape[0] // len(tiles)
    for j, (_, _, _, part) in enumerate(tiles):
        here = slice(j * tile, (j + 1) * tile)
        keys = part()
        kt_ref[:, here] = jnp.transpose(keys[:, 128:].astype(F32)).astype(BF)
        for b in range(blocks):
            at = slice(b * block, (b + 1) * block)
            scores = rows_by_rows(keys, q_ref[at, :])
            prob_ref[here, at] = jnp.exp2(scores * LOG2E - lse_ref[b][:1, :]).astype(BF)
        pltpu.make_async_copy(prob_ref.at[here], far_prob_ref.at[here], sems.at[j]).start()
    for j in range(len(tiles)):
        here = slice(j * tile, (j + 1) * tile)
        pltpu.make_async_copy(prob_ref.at[here], far_prob_ref.at[here], sems.at[j]).wait()


def branch_body(cot_ref, ahead_ref, behind_ref, conv_ref, out_ref):
    ring = 4
    place = lax.axis_index("seq") // (lax.axis_size("seq") // ring)
    out_ref[...] = (
        jnp.where(place < ring - 1, rows_by_rows(ahead_ref[...], conv_ref[0]), 0.0)
        + rows_by_rows(cot_ref[...], conv_ref[1])
        + jnp.where(place > 0, rows_by_rows(behind_ref[...], conv_ref[2]), 0.0)
    )


def gelu_pieces(wide):
    normal_cdf = 0.5 * (1.0 + lax.erf(wide * (1.0 / math.sqrt(2.0))))
    density = jnp.exp(-0.5 * wide * wide) * (1.0 / math.sqrt(2.0 * math.pi))
    return (wide * normal_cdf, normal_cdf + wide * density)


def middle_body(*refs):
    fars, (grad_ref, send_ref, *acts) = refs[:5], refs[5:11]
    recv_ref, proj_ref, stream_ref, cot_ref, branch_ref, att_ref, sems = refs[11:]
    arriving = [
        pltpu.make_async_copy(far, near, sems.at[i])
        for i, (far, near) in enumerate(
            zip(fars, (recv_ref, proj_ref, stream_ref, cot_ref, branch_ref))
        )
    ]
    for one in arriving:
        one.start()
    ring = len(acts)
    place = lax.axis_index("seq") // (lax.axis_size("seq") // ring)
    quarter = recv_ref.shape[1] // 3
    arriving[0].wait()
    for h in range(HEADS):
        for j in range(3):
            piece = recv_ref[h, j * quarter : (j + 1) * quarter, :].astype(F32)
            at = h * VAL + j * 64
            att_ref[:, at : at + 64] = on_top(piece, 4).astype(BF)
    for one in arriving[1:]:
        one.wait()
    inside = stream_ref[...].astype(F32) + plain(att_ref[...], proj_ref[...])
    activated, slope = gelu_pieces(inside.astype(BF).astype(F32))
    grad = (cot_ref[...].astype(F32) + slope * branch_ref[...]).astype(BF)
    grad_ref[...] = grad
    out_grad = rows_by_rows(grad, proj_ref[...])
    for h in range(HEADS):
        for j in range(3):
            at = h * VAL + j * 64
            piece = side_by_side(out_grad[:, at : at + 64], 4).astype(BF)
            send_ref[h, j * quarter : (j + 1) * quarter, :] = piece
    share = activated.shape[1] // ring
    blocks = [activated[:, k * share : (k + 1) * share].astype(BF) for k in range(ring)]
    for r, act_ref in enumerate(acts):
        block = blocks[0]
        for k in range(1, ring):
            block = jnp.where(lax.rem(place + r, ring) == k, blocks[k], block)
        act_ref[...] = block


def backward_body(*refs):
    far_recv, far_att, far_own, far_prob, far_kt, far_q, far_oth = refs[:7]
    far_own_out, far_oth_out = refs[7:9]
    recv_ref, att_ref, own_ref, prob_ref, kt_ref, q_ref, oth_ref = refs[9:16]
    own_out_ref, oth_out_ref, out_ref, grad_ref, turned_ref, sems = refs[16:]
    chips, rows, _ = oth_out_ref.shape
    mine = chips * rows
    quarter = rows // 4
    block = 512
    tiles = key_tiles(own_ref, oth_ref)
    tile = 2 * mine // len(tiles)
    heres = [slice(j * tile, (j + 1) * tile) for j in range(len(tiles))]
    recv, att, own, kt, query, oth = [
        pltpu.make_async_copy(far, near, sems.at[i])
        for i, (far, near) in enumerate(
            (
                (far_recv, recv_ref),
                (far_att, att_ref),
                (far_own, own_ref),
                (far_kt, kt_ref),
                (far_q, q_ref),
                (far_oth, oth_ref),
            )
        )
    ]
    probs = [
        pltpu.make_async_copy(far_prob.at[here], prob_ref.at[here], sems.at[6 + j])
        for j, here in enumerate(heres)
    ]
    leaving = []
    for j, (side, first, step, _) in enumerate(tiles):
        if side == 1:
            at = slice(first, first + step)
            leaving.append(
                pltpu.make_async_copy(oth_out_ref.at[at], far_oth_out.at[at], sems.at[8 + j])
            )
    leaving.append(pltpu.make_async_copy(own_out_ref, far_own_out, sems.at[12]))
    order = [2, 3, 0, 1]
    for one in (recv, att, oth, probs[2], query, kt, probs[3], own, probs[0], probs[1]):
        one.start()
    recv.wait()
    for c in range(chips):
        pieces = [
            on_top(recv_ref[c, j * quarter : (j + 1) * quarter, :].astype(F32), 4) for j in range(3)
        ]
        padded = jnp.concatenate([*pieces, jnp.zeros((rows, KEY), F32)], axis=1)
        out_ref[c * rows : (c + 1) * rows, :] = padded.astype(BF)
    att.wait()
    deltas = []
    for b in range(mine // block):
        at = slice(b * block, (b + 1) * block)
        each = out_ref[at, :].astype(F32) * att_ref[at, :].astype(F32)
        delta = jnp.sum(each, axis=1, keepdims=True)
        deltas.append(jnp.transpose(jnp.broadcast_to(delta, (block, 128)))[:1, :])

    def score_grads(j):
        probs[j].wait()
        keys = tiles[j][3]()
        for b, delta in enumerate(deltas):
            at = slice(b * block, (b + 1) * block)
            grads = rows_by_rows(keys, out_ref[at, :]) - delta
            grad_ref[j % 2, :, at] = (prob_ref[heres[j], at].astype(F32) * grads).astype(BF)

    oth.wait()
    score_grads(order[0])
    query.wait()
    kt.wait()
    for i, j in enumerate(order):
        side, first, step, _ = tiles[j]
        if i + 1 < len(order):
            if i + 1 == len(order) // 2:
                own.wait()
            score_grads(order[i + 1])
        slot = grad_ref[j % 2]
        summed = plain(prob_ref[heres[j], :], out_ref[...]) + plain(slot, q_ref[...])
        near = (own_out_ref, oth_out_ref)[side]
        near[first : first + step, :rows, :] = summed.astype(BF).reshape(step, rows, WIDE)
        if side == 1:
            leaving[i].start()
        turned = plain(kt_ref[:, heres[j]], slot)
        turned_ref[...] = turned if i == 0 else turned_ref[...] + turned
    scale = 1.0 / math.sqrt(KEY)
    for b in range(mine // 384):
        turned = jnp.transpose(turned_ref[:, b * 384 : (b + 1) * 384]) * scale
        for i in range(384 // rows):
            part = turned[i * rows : (i + 1) * rows, 64:]
            own_out_ref[b * (384 // rows) + i, rows:, :] = side_by_side(part, 4).astype(BF)
    leaving[-1].start()
    for one in leaving:
        one.wait()


def weight_body(*refs):
    ring = 4
    acts, cots, (out_ref, act_ref, cot_ref) = refs[:ring], refs[ring : 2 * ring], refs[2 * ring :]
    index = lax.axis_index("seq")
    stride = lax.axis_size("seq") // ring
    place, here = index // stride, index % stride
    rows, share = acts[0].shape
    for r in range(ring):
        at = pl.ds(pl.multiple_of(lax.rem(place + r, ring) * rows, rows), rows)
        act_ref[at, :] = acts[r][...]
        cot_ref[at, :] = cots[r][...]
    bins = ring * rows
    act = jnp.transpose(act_ref[...].astype(F32)).astype(BF)
    terms = (
        plain(act[:, : bins - rows], cot_ref[rows:, :]),
        plain(act, cot_ref[...]),
        plain(act[:, rows:], cot_ref[: bins - rows, :]),
    )
    piece = share // 4
    parts = [
        jnp.concatenate([t[g * piece : (g + 1) * piece] for t in terms], axis=0) for g in range(4)
    ]
    order = []
    for r in range(4):
        part = parts[r]
        for g in range(1, 4):
            part = jnp.where(here == g, parts[g ^ r], part)
        order.append(part)
    out_ref[...] = jnp.transpose(jnp.concatenate(order, axis=0)).astype(BF)


def sum_of(refs):
    both = refs[0][...].astype(F32)
    for ref in refs[1:]:
        both = both + ref[...].astype(F32)
    return both


def dp_sum_body(terms_ref, *outs):
    both = sum_of([terms_ref.at[i] for i in range(terms_ref.shape[0])])
    width = outs[0].shape[1]
    for r, out_ref in enumerate(outs):
        out_ref[...] = both[:, r * width : (r + 1) * width]


def last_sum_body(*refs):
    both = jnp.transpose(sum_of(refs[:4])) * (1.0 / lax.axis_size("dp"))
    rows = both.shape[0] // 3
    for t in range(3):
        refs[4][t] = both[t * rows : (t + 1) * rows]


def finish_body(recv_ref, q_ref, k_ref, v_ref):
    rows = q_ref.shape[0]
    for h in range(HEADS):
        v_ref[:, h * VAL : (h + 1) * VAL] = recv_ref[h, :rows, :VAL]
        k_ref[:, h * KEY : (h + 1) * KEY] = recv_ref[h, :rows, VAL:]
        q_ref[:, h * KEY : (h + 1) * KEY] = on_top(recv_ref[h, rows:, :].astype(F32), 4).astype(BF)


def shards(queries, key_rows, values, out_proj, stream, cotangent, conv_weight):
    count = lax.axis_size("seq")
    chips = count // 2
    rows = queries.shape[1]
    channels = cotangent.shape[2]
    mine = chips * rows
    same_core = [[2 * c + p for c in range(chips)] for p in range(2)]
    partner = [(i, i ^ 1) for i in range(count)]

    def shape(*dims, dtype=BF):
        return jax.ShapeDtypeStruct(dims, dtype)

    def exchange(value):
        return lax.all_to_all(value, "seq", 0, 0, axis_index_groups=same_core, tiled=True)

    def swap(value, bit=1):
        return lax.ppermute(value, "seq", [(i, i ^ bit) for i in range(count)])

    def round_ring(value, by):
        return lax.ppermute(value, "seq", [(i, (i - by) % count) for i in range(count)])

    ring = 4
    stride = count // ring
    copies = lax.axis_size("dp")
    block = 512
    pairs_done = mine * 2 * mine
    part, quarter = 3 * channels // count, rows // 4

    packed = call(
        pack_body,
        [shape(chips, rows + quarter, WIDE)],
        [
            pltpu.VMEM((rows, HEADS * VAL), BF),
            pltpu.VMEM((chips, rows + quarter, WIDE), BF),
            pltpu.SemaphoreType.DMA((HEADS + 1,)),
        ],
        60,
        0,
        2 * MIB,
        0,
        "pack",
        far_in=(2,),
        far_out=(0,),
    )(queries[0], key_rows[0], values[0])
    own, cot = lax.optimization_barrier((exchange(packed), cotangent[0]))
    oth = swap(own)
    ahead, behind = round_ring(cot, stride), round_ring(cot, 3 * stride)
    query, attended, lse, send = call(
        forward_body,
        [
            shape(mine, WIDE),
            shape(mine, WIDE),
            shape(mine // block, 8, block, dtype=F32),
            shape(chips, 3 * quarter, WIDE),
        ],
        [
            pltpu.VMEM((chips, rows + quarter, WIDE), BF),
            pltpu.VMEM((mine, WIDE), BF),
            pltpu.VMEM((mine, WIDE), BF),
            pltpu.SemaphoreType.DMA((2 + mine // block,)),
            *[pltpu.VMEM((block, 2 * mine), F32)] * 2,
        ],
        56,
        4 * pairs_done * WIDE,
        6 * MIB,
        pairs_done,
        "forward",
        far_in=(1,),
        far_out=(0, 1),
    )(own, oth)
    send, ahead, behind = lax.optimization_barrier((send, ahead, behind))
    recv = exchange(send)
    across = round_ring(ahead, stride)
    probs, keys_turned = call(
        probs_body,
        [shape(2 * mine, mine), shape(128, 2 * mine)],
        [pltpu.VMEM((2 * mine, mine), BF), pltpu.SemaphoreType.DMA((4,))],
        56,
        2 * pairs_done * WIDE,
        12 * MIB,
        pairs_done,
        "probs",
        far_out=(0,),
    )(own, oth, query, lse)
    branch = call(
        branch_body,
        [shape(rows, channels, dtype=F32)],
        [],
        56,
        6 * rows * channels * channels,
        5 * MIB,
        0,
        "branch",
    )(cot, ahead, behind, conv_weight)
    recv, branch = lax.optimization_barrier((recv, branch))
    ins = (recv, out_proj, stream[0], cot, branch)
    stream_grad, send, *acts = call(
        middle_body,
        [
            shape(rows, channels),
            shape(chips, 3 * quarter, WIDE),
            *[shape(rows, channels // ring)] * ring,
        ],
        [
            *[pltpu.VMEM(one.shape, one.dtype) for one in ins],
            pltpu.VMEM((rows, HEADS * VAL), BF),
            pltpu.SemaphoreType.DMA((5,)),
        ],
        56,
        4 * rows * channels * HEADS * VAL,
        5 * MIB,
        2 * rows * channels,
        "middle",
        far_in=range(5),
    )(*ins)
    recv = exchange(send)
    across, *acts = lax.optimization_barrier((across, *acts))
    moved = [round_ring(acts[ring - by], by * stride) for by in (1, 2, 3)]
    terms = call(
        weight_body,
        [shape(channels, ring * part)],
        [
            pltpu.VMEM((ring * rows, channels // ring), BF),
            pltpu.VMEM((ring * rows, channels), BF),
        ],
        56,
        6 * ring * rows * channels * channels // ring,
        5 * MIB,
        0,
        "weight",
    )(acts[0], *moved, cot, ahead, across, behind)
    recv, terms, probs, keys_turned = lax.optimization_barrier((recv, terms, probs, keys_turned))
    terms = terms.reshape(copies, channels // copies, ring * part)
    terms = lax.all_to_all(terms, "dp", 0, 0, tiled=True)
    ins = (recv, attended, own, probs, keys_turned, query, oth)
    own_grad, oth_grad = call(
        backward_body,
        [shape(chips, rows + quarter, WIDE), shape(chips, rows, WIDE)],
        [
            *[pltpu.VMEM(one.shape, one.dtype) for one in ins],
            pltpu.VMEM((chips, rows + quarter, WIDE), BF),
            pltpu.VMEM((chips, rows, WIDE), BF),
            pltpu.VMEM((mine, WIDE), BF),
            pltpu.VMEM((2, mine // 2, mine), BF),
            pltpu.VMEM((128, mine), F32),
            pltpu.SemaphoreType.DMA((13,)),
        ],
        56,
        8 * pairs_done * WIDE,
        16 * MIB,
        0,
        "backward",
        far_in=range(7),
        far_out=(0, 1),
    )(*ins)
    swapped = swap(oth_grad)
    swapped = jnp.pad(swapped.astype(F32), ((0, 0), (0, quarter), (0, 0)))
    packed = (own_grad.astype(F32) + swapped).astype(BF)
    packed, terms = lax.optimization_barrier((packed, terms))
    recv = exchange(packed)
    parts = call(
        dp_sum_body,
        [shape(channels // copies, part, dtype=F32)] * ring,
        [],
        12,
        0,
        MIB,
        0,
        "dp_sum",
    )(terms)
    parts = [parts[0]] + [swap(parts[r], r) for r in (1, 2, 3)]
    weight_grad = call(
        last_sum_body,
        [shape(3, channels // count, channels // copies, dtype=F32)],
        [],
        12,
        0,
        MIB,
        0,
        "last_sum",
    )(*parts)
    query_grad, key_grad, value_grad = call(
        finish_body,
        [shape(rows, HEADS * KEY), shape(rows, HEADS * KEY), shape(rows, HEADS * VAL)],
        [],
        12,
        0,
        2 * MIB,
        0,
        "finish",
    )(recv)
    return (query_grad[None], key_grad[None], value_grad[None], stream_grad[None], weight_grad)


def solution(mesh):
    return jax.shard_map(
        shards,
        mesh=mesh,
        in_specs=(
            P("dp", "seq", None),
            P("dp", "seq", None),
            P("dp", "seq", None),
            P(),
            P("dp", "seq", None),
            P("dp", "seq", None),
            P(),
        ),
        out_specs=(
            P("dp", "seq", None),
            P("dp", "seq", None),
            P("dp", "seq", None),
            P("dp", "seq", None),
            P(None, "seq", "dp"),
        ),
        check_vma=False,
    )
```

```python
import math

import jax
import jax.numpy as jnp
from jax import lax
from jax.experimental import pallas as pl
from jax.experimental.pallas import tpu as pltpu
from jax.sharding import PartitionSpec as P

HEADS = 8
KEY = 64
VAL = 192
WIDE = VAL + KEY
LOG2E = math.log2(math.e)
BF = jnp.bfloat16
F32 = jnp.float32
MIB = 1024 * 1024


def rows_by_rows(left, right):
    return lax.dot_general(left, right, (((1,), (1,)), ((), ())), preferred_element_type=F32)


def plain(left, right):
    return lax.dot_general(left, right, (((1,), (0,)), ((), ())), preferred_element_type=F32)


def call(body, outs, scratch, vmem_mib, flops, nbytes, exps, name, far_in=(), far_out=()):
    vmem = pl.BlockSpec(memory_space=pltpu.VMEM)
    far = pl.BlockSpec(memory_space=pl.ANY)
    outs = tuple(outs)

    def run(*arrays):
        got = pl.pallas_call(
            body,
            out_shape=outs,
            in_specs=[far if i in far_in else vmem for i in range(len(arrays))],
            out_specs=tuple(far if i in far_out else vmem for i in range(len(outs))),
            scratch_shapes=list(scratch),
            compiler_params=pltpu.CompilerParams(vmem_limit_bytes=vmem_mib * MIB),
            cost_estimate=pl.CostEstimate(flops=flops, bytes_accessed=nbytes, transcendentals=exps),
            name=name,
        )(*arrays)
        return got if len(outs) > 1 else got[0]

    return run


def side_by_side(block, parts):
    rows = block.shape[0] // parts
    return jnp.concatenate([block[i * rows : (i + 1) * rows] for i in range(parts)], axis=1)


def on_top(block, parts):
    width = block.shape[1] // parts
    return jnp.concatenate([block[:, i * width : (i + 1) * width] for i in range(parts)], axis=0)


def pack_body(q_ref, k_ref, v_ref, out_ref):
    rows = q_ref.shape[0]
    for h in range(HEADS):
        out_ref[h, :rows, :VAL] = v_ref[:, h * VAL : (h + 1) * VAL]
        out_ref[h, :rows, VAL:] = k_ref[:, h * KEY : (h + 1) * KEY]
        part = q_ref[:, h * KEY : (h + 1) * KEY].astype(F32) * (1.0 / math.sqrt(KEY))
        out_ref[h, rows:, :] = side_by_side(part, 4).astype(BF)


def key_tiles(own_ref, oth_ref, count=2):
    chips = own_ref.shape[0]
    rows, step = own_ref.shape[1] * 4 // 5, chips // count
    return [
        (
            side,
            t * step,
            step,
            lambda r=ref, t=t: r[t * step : (t + 1) * step, :rows, :].reshape(step * rows, WIDE),
        )
        for side, ref in enumerate((own_ref, oth_ref))
        for t in range(count)
    ]


def forward_body(own_ref, oth_ref, q_ref, att_ref, lse_ref, send_ref, *score_refs):
    block = score_refs[0].shape[0]
    chips = own_ref.shape[0]
    rows = own_ref.shape[1] * 4 // 5
    mine = chips * rows
    blocks = mine // block
    for c in range(chips):
        query = on_top(own_ref[c, rows:, :].astype(F32), 4)
        padded = jnp.concatenate([jnp.zeros((rows, VAL), F32), query], axis=1)
        q_ref[c * rows : (c + 1) * rows, :] = padded.astype(BF)
    tiles = key_tiles(own_ref, oth_ref)
    tile = 2 * mine // len(tiles)

    def score(b, j, top):
        scores = rows_by_rows(q_ref[b * block : (b + 1) * block, :], tiles[j][3]())
        score_refs[b % 2][:, j * tile : (j + 1) * tile] = scores
        high = jnp.max(scores, axis=1, keepdims=True)
        return high if top is None else jnp.maximum(top, high)

    top = None
    for j in range(len(tiles)):
        top = score(0, j, top)
    for b in range(blocks):
        following = None
        top = top * LOG2E
        total = jnp.zeros((block, 1), F32)
        summed = jnp.zeros((block, WIDE), F32)
        for j, (_, _, _, part) in enumerate(tiles):
            if b + 1 < blocks:
                following = score(b + 1, j, following)
            expo = jnp.exp2(score_refs[b % 2][:, j * tile : (j + 1) * tile] * LOG2E - top)
            total = total + jnp.sum(expo, axis=1, keepdims=True)
            summed = summed + plain(expo.astype(BF), part())
        att_ref[b * block : (b + 1) * block, :] = (summed * (1.0 / total)).astype(BF)
        turned = jnp.transpose(jnp.broadcast_to(top + jnp.log2(total), (block, 128)))
        lse_ref[b] = turned[:8, :]
        top = following
    for c in range(chips):
        part = att_ref[c * rows : (c + 1) * rows, :].astype(F32)
        for j in range(3):
            piece = side_by_side(part[:, j * 64 : (j + 1) * 64], 4).astype(BF)
            send_ref[c, j * (rows // 4) : (j + 1) * (rows // 4), :] = piece


def probs_body(own_ref, oth_ref, q_ref, lse_ref, far_prob_ref, kt_ref, prob_ref, sems):
    blocks, _, block = lse_ref.shape
    tiles = key_tiles(own_ref, oth_ref)
    tile = prob_ref.shape[0] // len(tiles)
    for j, (_, _, _, part) in enumerate(tiles):
        here = slice(j * tile, (j + 1) * tile)
        keys = part()
        kt_ref[:, here] = jnp.transpose(keys[:, 128:].astype(F32)).astype(BF)
        for b in range(blocks):
            at = slice(b * block, (b + 1) * block)
            scores = rows_by_rows(keys, q_ref[at, :])
            prob_ref[here, at] = jnp.exp2(scores * LOG2E - lse_ref[b][:1, :]).astype(BF)
        pltpu.make_async_copy(prob_ref.at[here], far_prob_ref.at[here], sems.at[j]).start()
    for j in range(len(tiles)):
        here = slice(j * tile, (j + 1) * tile)
        pltpu.make_async_copy(prob_ref.at[here], far_prob_ref.at[here], sems.at[j]).wait()


def branch_body(cot_ref, ahead_ref, behind_ref, conv_ref, out_ref):
    ring = 4
    place = lax.axis_index("seq") // (lax.axis_size("seq") // ring)
    out_ref[...] = (
        jnp.where(place < ring - 1, rows_by_rows(ahead_ref[...], conv_ref[0]), 0.0)
        + rows_by_rows(cot_ref[...], conv_ref[1])
        + jnp.where(place > 0, rows_by_rows(behind_ref[...], conv_ref[2]), 0.0)
    )


def gelu_pieces(wide):
    normal_cdf = 0.5 * (1.0 + lax.erf(wide * (1.0 / math.sqrt(2.0))))
    density = jnp.exp(-0.5 * wide * wide) * (1.0 / math.sqrt(2.0 * math.pi))
    return (wide * normal_cdf, normal_cdf + wide * density)


def middle_body(*refs):
    fars, (grad_ref, send_ref, *acts) = refs[:5], refs[5:11]
    recv_ref, proj_ref, stream_ref, cot_ref, branch_ref, att_ref, sems = refs[11:]
    arriving = [
        pltpu.make_async_copy(far, near, sems.at[i])
        for i, (far, near) in enumerate(
            zip(fars, (recv_ref, proj_ref, stream_ref, cot_ref, branch_ref))
        )
    ]
    for one in arriving:
        one.start()
    ring = len(acts)
    place = lax.axis_index("seq") // (lax.axis_size("seq") // ring)
    quarter = recv_ref.shape[1] // 3
    arriving[0].wait()
    for h in range(HEADS):
        for j in range(3):
            piece = recv_ref[h, j * quarter : (j + 1) * quarter, :].astype(F32)
            at = h * VAL + j * 64
            att_ref[:, at : at + 64] = on_top(piece, 4).astype(BF)
    for one in arriving[1:]:
        one.wait()
    inside = stream_ref[...].astype(F32) + plain(att_ref[...], proj_ref[...])
    activated, slope = gelu_pieces(inside.astype(BF).astype(F32))
    grad = (cot_ref[...].astype(F32) + slope * branch_ref[...]).astype(BF)
    grad_ref[...] = grad
    out_grad = rows_by_rows(grad, proj_ref[...])
    for h in range(HEADS):
        for j in range(3):
            at = h * VAL + j * 64
            piece = side_by_side(out_grad[:, at : at + 64], 4).astype(BF)
            send_ref[h, j * quarter : (j + 1) * quarter, :] = piece
    share = activated.shape[1] // ring
    blocks = [activated[:, k * share : (k + 1) * share].astype(BF) for k in range(ring)]
    for r, act_ref in enumerate(acts):
        block = blocks[0]
        for k in range(1, ring):
            block = jnp.where(lax.rem(place + r, ring) == k, blocks[k], block)
        act_ref[...] = block


def backward_body(*refs):
    far_recv, far_att, far_own, far_prob, far_kt, far_q, far_oth = refs[:7]
    far_own_out, far_oth_out = refs[7:9]
    recv_ref, att_ref, own_ref, prob_ref, kt_ref, q_ref, oth_ref = refs[9:16]
    own_out_ref, oth_out_ref, out_ref, grad_ref, turned_ref, sems = refs[16:]
    chips, rows, _ = oth_out_ref.shape
    mine = chips * rows
    quarter = rows // 4
    block = 512
    tiles = key_tiles(own_ref, oth_ref)
    tile = 2 * mine // len(tiles)
    heres = [slice(j * tile, (j + 1) * tile) for j in range(len(tiles))]
    recv, att, own, kt, query, oth = [
        pltpu.make_async_copy(far, near, sems.at[i])
        for i, (far, near) in enumerate(
            (
                (far_recv, recv_ref),
                (far_att, att_ref),
                (far_own, own_ref),
                (far_kt, kt_ref),
                (far_q, q_ref),
                (far_oth, oth_ref),
            )
        )
    ]
    probs = [
        pltpu.make_async_copy(far_prob.at[here], prob_ref.at[here], sems.at[6 + j])
        for j, here in enumerate(heres)
    ]
    leaving = []
    for j, (side, first, step, _) in enumerate(tiles):
        if side == 1:
            at = slice(first, first + step)
            leaving.append(
                pltpu.make_async_copy(oth_out_ref.at[at], far_oth_out.at[at], sems.at[8 + j])
            )
    leaving.append(pltpu.make_async_copy(own_out_ref, far_own_out, sems.at[12]))
    order = [2, 3, 0, 1]
    for one in (recv, att, oth, probs[2], query, kt, probs[3], own, probs[0], probs[1]):
        one.start()
    recv.wait()
    for c in range(chips):
        pieces = [
            on_top(recv_ref[c, j * quarter : (j + 1) * quarter, :].astype(F32), 4) for j in range(3)
        ]
        padded = jnp.concatenate([*pieces, jnp.zeros((rows, KEY), F32)], axis=1)
        out_ref[c * rows : (c + 1) * rows, :] = padded.astype(BF)
    att.wait()
    deltas = []
    for b in range(mine // block):
        at = slice(b * block, (b + 1) * block)
        each = out_ref[at, :].astype(F32) * att_ref[at, :].astype(F32)
        delta = jnp.sum(each, axis=1, keepdims=True)
        deltas.append(jnp.transpose(jnp.broadcast_to(delta, (block, 128)))[:1, :])

    def score_grads(j):
        probs[j].wait()
        keys = tiles[j][3]()
        for b, delta in enumerate(deltas):
            at = slice(b * block, (b + 1) * block)
            grads = rows_by_rows(keys, out_ref[at, :]) - delta
            grad_ref[j % 2, :, at] = (prob_ref[heres[j], at].astype(F32) * grads).astype(BF)

    oth.wait()
    score_grads(order[0])
    query.wait()
    kt.wait()
    for i, j in enumerate(order):
        side, first, step, _ = tiles[j]
        if i + 1 < len(order):
            if i + 1 == len(order) // 2:
                own.wait()
            score_grads(order[i + 1])
        slot = grad_ref[j % 2]
        summed = plain(prob_ref[heres[j], :], out_ref[...]) + plain(slot, q_ref[...])
        near = (own_out_ref, oth_out_ref)[side]
        near[first : first + step, :rows, :] = summed.astype(BF).reshape(step, rows, WIDE)
        if side == 1:
            leaving[i].start()
        turned = plain(kt_ref[:, heres[j]], slot)
        turned_ref[...] = turned if i == 0 else turned_ref[...] + turned
    scale = 1.0 / math.sqrt(KEY)
    for b in range(mine // 384):
        turned = jnp.transpose(turned_ref[:, b * 384 : (b + 1) * 384]) * scale
        for i in range(384 // rows):
            part = turned[i * rows : (i + 1) * rows, 64:]
            own_out_ref[b * (384 // rows) + i, rows:, :] = side_by_side(part, 4).astype(BF)
    leaving[-1].start()
    for one in leaving:
        one.wait()


def weight_body(*refs):
    ring = 4
    acts, cots, (out_ref, act_ref, cot_ref) = refs[:ring], refs[ring : 2 * ring], refs[2 * ring :]
    index = lax.axis_index("seq")
    stride = lax.axis_size("seq") // ring
    place, here = index // stride, index % stride
    rows, share = acts[0].shape
    for r in range(ring):
        at = pl.ds(pl.multiple_of(lax.rem(place + r, ring) * rows, rows), rows)
        act_ref[at, :] = acts[r][...]
        cot_ref[at, :] = cots[r][...]
    bins = ring * rows
    act = jnp.transpose(act_ref[...].astype(F32)).astype(BF)
    terms = (
        plain(act[:, : bins - rows], cot_ref[rows:, :]),
        plain(act, cot_ref[...]),
        plain(act[:, rows:], cot_ref[: bins - rows, :]),
    )
    piece = share // 4
    parts = [
        jnp.concatenate([t[g * piece : (g + 1) * piece] for t in terms], axis=0) for g in range(4)
    ]
    order = []
    for r in range(4):
        part = parts[r]
        for g in range(1, 4):
            part = jnp.where(here == g, parts[g ^ r], part)
        order.append(part)
    out_ref[...] = jnp.transpose(jnp.concatenate(order, axis=0)).astype(BF)


def sum_of(refs):
    both = refs[0][...].astype(F32)
    for ref in refs[1:]:
        both = both + ref[...].astype(F32)
    return both


def dp_sum_body(terms_ref, *outs):
    both = sum_of([terms_ref.at[i] for i in range(terms_ref.shape[0])])
    width = outs[0].shape[1]
    for r, out_ref in enumerate(outs):
        out_ref[...] = both[:, r * width : (r + 1) * width]


def last_sum_body(*refs):
    both = jnp.transpose(sum_of(refs[:4])) * (1.0 / lax.axis_size("dp"))
    rows = both.shape[0] // 3
    for t in range(3):
        refs[4][t] = both[t * rows : (t + 1) * rows]


def add_body(own_ref, recv_ref, out_ref):
    rows = recv_ref.shape[1]
    for c in range(own_ref.shape[0]):
        both = own_ref[c, :rows, :].astype(F32) + recv_ref[c].astype(F32)
        out_ref[c, :rows, :] = both.astype(BF)
        out_ref[c, rows:, :] = own_ref[c, rows:, :]


def finish_body(recv_ref, q_ref, k_ref, v_ref):
    rows = q_ref.shape[0]
    for h in range(HEADS):
        v_ref[:, h * VAL : (h + 1) * VAL] = recv_ref[h, :rows, :VAL]
        k_ref[:, h * KEY : (h + 1) * KEY] = recv_ref[h, :rows, VAL:]
        q_ref[:, h * KEY : (h + 1) * KEY] = on_top(recv_ref[h, rows:, :].astype(F32), 4).astype(BF)


def shards(queries, key_rows, values, out_proj, stream, cotangent, conv_weight):
    count = lax.axis_size("seq")
    chips = count // 2
    rows = queries.shape[1]
    channels = cotangent.shape[2]
    mine = chips * rows
    same_core = [[2 * c + p for c in range(chips)] for p in range(2)]
    partner = [(i, i ^ 1) for i in range(count)]

    def shape(*dims, dtype=BF):
        return jax.ShapeDtypeStruct(dims, dtype)

    def exchange(value):
        return lax.all_to_all(value, "seq", 0, 0, axis_index_groups=same_core, tiled=True)

    def swap(value, bit=1):
        return lax.ppermute(value, "seq", [(i, i ^ bit) for i in range(count)])

    def round_ring(value, by):
        return lax.ppermute(value, "seq", [(i, (i - by) % count) for i in range(count)])

    ring = 4
    stride = count // ring
    copies = lax.axis_size("dp")
    block = 512
    pairs_done = mine * 2 * mine
    part, quarter = 3 * channels // count, rows // 4

    packed = call(pack_body, [shape(chips, rows + quarter, WIDE)], [], 60, 0, 2 * MIB, 0, "pack")(
        queries[0], key_rows[0], values[0]
    )
    own, cot = lax.optimization_barrier((exchange(packed), cotangent[0]))
    oth = swap(own)
    ahead, behind = round_ring(cot, stride), round_ring(cot, 3 * stride)
    query, attended, lse, send = call(
        forward_body,
        [
            shape(mine, WIDE),
            shape(mine, WIDE),
            shape(mine // block, 8, block, dtype=F32),
            shape(chips, 3 * quarter, WIDE),
        ],
        [pltpu.VMEM((block, 2 * mine), F32)] * 2,
        36,
        4 * pairs_done * WIDE,
        6 * MIB,
        pairs_done,
        "forward",
    )(own, oth)
    send, ahead, behind = lax.optimization_barrier((send, ahead, behind))
    recv = exchange(send)
    across = round_ring(ahead, stride)
    probs, keys_turned = call(
        probs_body,
        [shape(2 * mine, mine), shape(128, 2 * mine)],
        [pltpu.VMEM((2 * mine, mine), BF), pltpu.SemaphoreType.DMA((4,))],
        56,
        2 * pairs_done * WIDE,
        12 * MIB,
        pairs_done,
        "probs",
        far_out=(0,),
    )(own, oth, query, lse)
    branch = call(
        branch_body,
        [shape(rows, channels, dtype=F32)],
        [],
        56,
        6 * rows * channels * channels,
        5 * MIB,
        0,
        "branch",
    )(cot, ahead, behind, conv_weight)
    recv, branch = lax.optimization_barrier((recv, branch))
    ins = (recv, out_proj, stream[0], cot, branch)
    stream_grad, send, *acts = call(
        middle_body,
        [
            shape(rows, channels),
            shape(chips, 3 * quarter, WIDE),
            *[shape(rows, channels // ring)] * ring,
        ],
        [
            *[pltpu.VMEM(one.shape, one.dtype) for one in ins],
            pltpu.VMEM((rows, HEADS * VAL), BF),
            pltpu.SemaphoreType.DMA((5,)),
        ],
        56,
        4 * rows * channels * HEADS * VAL,
        5 * MIB,
        2 * rows * channels,
        "middle",
        far_in=range(5),
    )(*ins)
    recv = exchange(send)
    across, *acts = lax.optimization_barrier((across, *acts))
    moved = [round_ring(acts[ring - by], by * stride) for by in (1, 2, 3)]
    terms = call(
        weight_body,
        [shape(channels, ring * part)],
        [
            pltpu.VMEM((ring * rows, channels // ring), BF),
            pltpu.VMEM((ring * rows, channels), BF),
        ],
        56,
        6 * ring * rows * channels * channels // ring,
        5 * MIB,
        0,
        "weight",
    )(acts[0], *moved, cot, ahead, across, behind)
    recv, terms, probs, keys_turned = lax.optimization_barrier((recv, terms, probs, keys_turned))
    terms = terms.reshape(copies, channels // copies, ring * part)
    terms = lax.all_to_all(terms, "dp", 0, 0, tiled=True)
    ins = (recv, attended, own, probs, keys_turned, query, oth)
    own_grad, oth_grad = call(
        backward_body,
        [shape(chips, rows + quarter, WIDE), shape(chips, rows, WIDE)],
        [
            *[pltpu.VMEM(one.shape, one.dtype) for one in ins],
            pltpu.VMEM((chips, rows + quarter, WIDE), BF),
            pltpu.VMEM((chips, rows, WIDE), BF),
            pltpu.VMEM((mine, WIDE), BF),
            pltpu.VMEM((2, mine // 2, mine), BF),
            pltpu.VMEM((128, mine), F32),
            pltpu.SemaphoreType.DMA((13,)),
        ],
        56,
        8 * pairs_done * WIDE,
        16 * MIB,
        0,
        "backward",
        far_in=range(7),
        far_out=(0, 1),
    )(*ins)
    swapped = swap(oth_grad)
    packed = call(add_body, [shape(chips, rows + quarter, WIDE)], [], 12, 0, 3 * MIB, 0, "add")(
        own_grad, swapped
    )
    packed, terms = lax.optimization_barrier((packed, terms))
    recv = exchange(packed)
    parts = call(
        dp_sum_body,
        [shape(channels // copies, part, dtype=F32)] * ring,
        [],
        12,
        0,
        MIB,
        0,
        "dp_sum",
    )(terms)
    parts = [parts[0]] + [swap(parts[r], r) for r in (1, 2, 3)]
    weight_grad = call(
        last_sum_body,
        [shape(3, channels // count, channels // copies, dtype=F32)],
        [],
        12,
        0,
        MIB,
        0,
        "last_sum",
    )(*parts)
    query_grad, key_grad, value_grad = call(
        finish_body,
        [shape(rows, HEADS * KEY), shape(rows, HEADS * KEY), shape(rows, HEADS * VAL)],
        [],
        12,
        0,
        2 * MIB,
        0,
        "finish",
    )(recv)
    return (query_grad[None], key_grad[None], value_grad[None], stream_grad[None], weight_grad)


def solution(mesh):
    return jax.shard_map(
        shards,
        mesh=mesh,
        in_specs=(
            P("dp", "seq", None),
            P("dp", "seq", None),
            P("dp", "seq", None),
            P(),
            P("dp", "seq", None),
            P("dp", "seq", None),
            P(),
        ),
        out_specs=(
            P("dp", "seq", None),
            P("dp", "seq", None),
            P("dp", "seq", None),
            P("dp", "seq", None),
            P(None, "seq", "dp"),
        ),
        check_vma=False,
    )
```
